256 devices in a mesh: freq: 16 (over z, core), tile: 16 (over x, y).
Axes of the slice: x: 4, y: 4, z: 8, core: 2. Of those that a mesh axis runs over, the one named last changes fastest.
Arguments:
- x_in: float32 [16, 2, 2304, 512], P('freq', None, 'tile'), may hold values from -6 to 6
- v_bases: float32 [16, 16, 2, 96, 2304], P('freq', None, None, None, 'tile'), may hold values from -0.375 to 0.375
- u_bases: float32 [16, 16, 2, 96, 8192], P('freq', None, None, None, 'tile'), may hold values from -0.109375 to 0.109375
- ranks: int32 [16, 16, 16], P('freq'), may hold values from 64 to 96, as said below
- mute: int32 [16, 512, 512], P('tile', 'freq'), may hold values from 64 to 512
Outputs:
- muted: float32 [16, 16, 2, 512, 512], P('tile', None, None, 'freq')
The draws below stay inside these ranges and needn't reach their ends.
Inputs may be any that keep to these rules, and one draw needn't show every extreme that they name: `ranks`: every frequency has a tile of rank 64 and tiles of rank 96.
All inputs are finite; a program needn't handle non-finite values.
Results may differ from the reference program's by a relative error of at most 0.0003.
Values sent between devices are 32-bit elements; how exact they have to be, the bound alone decides.
No kernel may reach another device: no remote copies, remote signals or barrier semaphores. Data moves between devices by JAX's collectives and lax.ppermute only.
A program may use at most 128 MiB of HBM per device.

```python
import math
import jax
import jax.numpy as jnp
from jax import lax

TILE_REC = 512
TILE_SRC = 144
RMAX = 96
RMIN = 64
NT = 512
FLOW = 20
FSTEP = 4
VP = 512
NTR = 16
NTC = 16
NR = 8192
NS = 2304
FREQS = 16


def draw_ranks(key, part):
    base_key = jax.random.fold_in(key, 7301)
    drawn = jax.random.randint(base_key, (FREQS, NTR, NTC), RMIN, RMAX + 1, dtype=jnp.int32)
    diagonal = (jnp.arange(NTR)[:, None] == jnp.arange(NTC)[None, :])[None, :, :]
    drawn = jnp.where(diagonal, jnp.int32(RMAX), drawn)
    corner = ((jnp.arange(NTR)[:, None] == 0) & (jnp.arange(NTC)[None, :] == NTC - 1))[None, :, :]
    drawn = jnp.where(corner, jnp.int32(RMIN), drawn)
    return drawn.astype(jnp.int32)


def with_ends(array, stream_key, least, top_value):
    spot = [jax.random.randint(jax.random.fold_in(stream_key, axis), (), 0, length) for axis, length in enumerate(array.shape)]
    longest = array.shape.index(max(array.shape))
    neighbour = spot[:longest] + [(spot[longest] + 1) % array.shape[longest]] + spot[longest + 1:]
    return array.at[tuple(spot)].set(least).at[tuple(neighbour)].set(top_value)


def shard_levels(key, extent, pieces, low, top_value):
    def one(dim, parts):
        heights = jax.random.uniform(jax.random.fold_in(jax.random.fold_in(key, 6), dim), (parts,), jnp.float32, low / len(pieces), top_value / len(pieces))
        return jnp.repeat(jnp.exp(heights), extent[dim] // parts).reshape((-1,) + (1,) * (len(extent) - dim - 1))

    level = one(*pieces[0])
    for cut in pieces[1:]:
        level = level * one(*cut)
    return level


def centred(rng, shape, deviation, reach, cuts=(), kind=jnp.bfloat16):
    level = shard_levels(rng, shape, cuts, -0.22, 0.18) if cuts else 1.0
    entries = jax.random.normal(rng, shape, jnp.float32) * deviation * level
    return jnp.minimum(jnp.maximum(entries, -reach), reach).astype(kind)


def setup_inputs(seed: int = 0) -> dict:
    key_of = jax.random.split(jax.random.key(seed), 6)
    return {
        "x_in": centred(key_of[0], (FREQS, 2, NS, VP), 1.0, 6.0, ((0, 16), (2, 16)), jnp.float32),
        "v_bases": centred(key_of[1], (FREQS, NTR, 2, RMAX, NS), (2 * TILE_SRC) ** -0.5, 0.375, ((0, 16), (4, 16)), jnp.float32),
        "u_bases": centred(key_of[2], (FREQS, NTC, 2, RMAX, NR), (2 * NTC * RMAX) ** -0.5, 0.109375, ((0, 16), (4, 16)), jnp.float32),
        "ranks": draw_ranks(jax.random.fold_in(key_of[5], 71), 0),
        "mute": with_ends(jax.random.randint(key_of[4], (NTR, TILE_REC, VP), NT // 8, NT + 1), jax.random.fold_in(key_of[4], 1), NT // 8, NT).astype(jnp.int32),
    }


def time_mute(spectra, mute_row):
    freq_count = spectra.shape[0]
    highest = lax.Precision.HIGHEST
    sample_index = jnp.arange(NT, dtype=jnp.int32)
    freq_bins = FLOW + FSTEP * jnp.arange(freq_count, dtype=jnp.int32)
    phases = (sample_index[:, None] * freq_bins[None, :]) % NT
    angles = phases.astype(jnp.float32) * (2.0 * math.pi / NT)
    cosine = jnp.cos(angles)
    sine_table = jnp.sin(angles)
    forward = jnp.stack([cosine, -sine_table], axis=2).reshape(NT, 2 * freq_count)
    inverse = forward * (2.0 / NT)
    flat = spectra.reshape(2 * freq_count, -1)
    series = jnp.dot(inverse, flat, precision=highest)
    mute_flat = mute_row.reshape(1, -1)
    series = jnp.where(sample_index[:, None] < mute_flat, series, jnp.zeros_like(series))
    result = jnp.dot(forward.T, series, precision=highest)
    return result.reshape(spectra.shape)


def one_frequency(operands):
    wave, vbase, ubase, rank_table = operands
    highest = lax.Precision.HIGHEST
    wave_tiles = wave.reshape(2, NTC, TILE_SRC, VP)
    vbase_tiles = vbase.reshape(NTR, 2, RMAX, NTC, TILE_SRC)

    def contract_v(first_op, second_op):
        return jnp.einsum('irjs,jsp->ijrp', first_op, second_op, precision=highest)

    coef_real = contract_v(vbase_tiles[:, 0], wave_tiles[0]) + contract_v(vbase_tiles[:, 1], wave_tiles[1])
    coef_imag = contract_v(vbase_tiles[:, 0], wave_tiles[1]) - contract_v(vbase_tiles[:, 1], wave_tiles[0])
    live_mask = (jnp.arange(RMAX, dtype=jnp.int32)[None, None, :] < rank_table[:, :, None]).astype(jnp.float32)
    coef_real = coef_real * live_mask[..., None]
    coef_imag = coef_imag * live_mask[..., None]
    ubase_tiles = ubase.reshape(NTC, 2, RMAX, NTR, TILE_REC)

    def contract_u(first_op, second_op):
        return jnp.einsum('jrin,ijrp->inp', first_op, second_op, precision=highest)

    field_real = contract_u(ubase_tiles[:, 0], coef_real) - contract_u(ubase_tiles[:, 1], coef_imag)
    field_imag = contract_u(ubase_tiles[:, 0], coef_imag) + contract_u(ubase_tiles[:, 1], coef_real)
    return jnp.stack([field_real, field_imag], axis=1)


def reference(x_in, v_bases, u_bases, ranks, mute):
    fields = lax.map(one_frequency, (x_in, v_bases, u_bases, ranks))
    by_row = jnp.moveaxis(fields, 1, 0)

    def transform(operands):
        spectra, mute_row = operands
        return time_mute(spectra, mute_row)

    return lax.map(transform, (by_row, mute))
```

```python
import functools
import math

import jax
import jax.numpy as jnp
import numpy as np
from jax import lax
from jax.experimental import pallas as pl
from jax.experimental.pallas import tpu as pltpu
from jax.sharding import PartitionSpec as P

NT = 512
FLOW = 20
FSTEP = 4
PERIOD = NT // FSTEP
GROUP = 8
SIDE = 4
RING = 8
LANES = 128
WIDTHS = (256, 256)


def split(value):
    high = value.astype(jnp.bfloat16)
    low = (value - high.astype(jnp.float32)).astype(jnp.bfloat16)
    return high, low


def dot(left, right):
    return jnp.dot(left, right, preferred_element_type=jnp.float32)


def dot_split(left, right):
    return dot(left[0], right[0]) + (dot(left[0], right[1]) + dot(left[1], right[0]))


def call(kernel, name, out_shape, flops=0, moved=1 << 20, limit=40, **kwargs):
    return pl.pallas_call(
        kernel,
        out_shape=out_shape,
        name=name,
        compiler_params=pltpu.CompilerParams(vmem_limit_bytes=limit << 20),
        cost_estimate=pl.CostEstimate(flops=flops, bytes_accessed=moved, transcendentals=0),
        **kwargs,
    )


def place_of_device():
    tile = lax.axis_index("tile")
    freq = lax.axis_index("freq")
    core = freq % 2
    straight = core == 0
    high, low = tile // SIDE, tile % SIDE
    values = (
        jnp.where(straight, high, low),
        jnp.where(straight, low, high),
        jnp.where(straight, SIDE, 1),
        jnp.where(straight, 1, SIDE),
        core,
        freq // 2,
        tile,
    )
    slot = lax.broadcasted_iota(jnp.int32, (8,), 0)
    place = jnp.zeros((8,), jnp.int32)
    for index, value in enumerate(values):
        place = jnp.where(slot == index, value.astype(jnp.int32), place)
    return place


def tile_at(place, first, second):
    return ((place[0] + first) & (SIDE - 1)) * place[2] + ((place[1] + second) & (SIDE - 1)) * place[3]


def plane_shift(array, first, second):
    pairs = []
    for freq in range(2 * RING):
        strides = (SIDE, 1) if freq % 2 == 0 else (1, SIDE)
        for one in range(SIDE):
            for two in range(SIDE):
                source = one * strides[0] + two * strides[1]
                target = (one + first) % SIDE * strides[0] + (two + second) % SIDE * strides[1]
                pairs.append((freq * SIDE * SIDE + source, freq * SIDE * SIDE + target))
    return lax.ppermute(array, ("freq", "tile"), pairs)


def ring_shift(array, step, swap):
    pairs = [
        (z * 2 + core, (z + step) % RING * 2 + (core + swap) % 2)
        for z in range(RING)
        for core in range(2)
    ]
    return lax.ppermute(array, "freq", pairs)


def pack_kernel(place, *refs):
    tiles, x_ref, out = refs[:SIDE], refs[SIDE], refs[SIDE + 1]
    ranks = tiles[0].shape[4]
    blocks = [tile[0, 0, part].T for tile in tiles for part in range(2)]
    out[:ranks] = jnp.concatenate(blocks, axis=1)
    span = out.shape[1] // SIDE
    rows = span * LANES // out.shape[1]
    wave = x_ref[0].reshape(span, -1)
    for column in range(wave.shape[1] // LANES):
        part = wave[:, LANES * column : LANES * (column + 1)]
        pieces = [part[start : start + rows] for start in range(0, span, rows)]
        base = ranks + rows * column
        out[base : base + rows] = jnp.concatenate(pieces, axis=1)


def pack(place, v_bases, x_in, first):
    _, _, parts, sources, ranks = v_bases.shape
    width = SIDE * parts * sources
    rows = ranks + parts * sources * WIDTHS[0] // width
    tile_spec = lambda second: pl.BlockSpec(
        (1, 1, parts, sources, ranks), lambda i, place: (0, tile_at(place, first, second), 0, 0, 0)
    )
    return call(
        pack_kernel,
        f"pack_{first}",
        jax.ShapeDtypeStruct((rows, width), jnp.float32),
        grid_spec=pltpu.PrefetchScalarGridSpec(
            num_scalar_prefetch=1,
            grid=(1,),
            in_specs=[tile_spec(second) for second in range(SIDE)]
            + [pl.BlockSpec((1, parts, sources, WIDTHS[0]), lambda i, place: (0, 0, 0, 0))],
            out_specs=pl.BlockSpec((rows, width), lambda i, place: (0, 0)),
        ),
    )(place, *[v_bases] * SIDE, x_in)


def coefficient_kernel(ranks, *refs):
    packed = refs[:SIDE]
    waves = refs[SIDE:-SIDE]
    outs = refs[-SIDE:]
    for first in range(SIDE):
        rows = packed[first][...]
        span = rows.shape[1] // SIDE
        if waves:
            wave = waves[first][...].reshape(span, -1)
        else:
            height = span * LANES // rows.shape[1]
            columns = []
            for base in range(ranks, rows.shape[0], height):
                tail = rows[base : base + height]
                pieces = [tail[:, at : at + LANES] for at in range(0, rows.shape[1], LANES)]
                columns.append(jnp.concatenate(pieces, axis=0))
            wave = jnp.concatenate(columns, axis=1)
        real, imag = wave[: span // 2], wave[span // 2 :]
        right = jnp.concatenate(
            [jnp.concatenate([real, imag], axis=1), jnp.concatenate([imag, -real], axis=1)], axis=0
        )
        left = jnp.concatenate(
            [rows[:ranks, span * second : span * (second + 1)] for second in range(SIDE)], axis=0
        )
        result = dot_split(split(left), split(right))
        for second in range(SIDE):
            outs[second][first] = result[ranks * second : ranks * (second + 1)]


def coefficients(packed, waves, ranks, start, width):
    rows, span = packed[0].shape
    sources = span // SIDE
    in_specs = [pl.BlockSpec((rows, span), lambda i: (0, 0))] * SIDE
    if waves:
        block = start // width
        in_specs += [pl.BlockSpec((2, sources // 2, width), lambda i: (0, 0, block))] * SIDE
    shape = (SIDE, ranks, 2 * width)
    return call(
        functools.partial(coefficient_kernel, ranks),
        f"coefficients_{width}",
        [jax.ShapeDtypeStruct(shape, jnp.float32)] * SIDE,
        flops=2 * 3 * SIDE * SIDE * ranks * sources * 2 * width,
        moved=4 << 20,
        grid=(1,),
        in_specs=in_specs,
        out_specs=[pl.BlockSpec(shape, lambda i: (0, 0, 0))] * SIDE,
    )(*packed, *waves)


def bases_kernel(place, rank_table, *refs):
    tiles, high, low = refs[:SIDE], refs[SIDE], refs[SIDE + 1]
    second = pl.program_id(0)
    for part in range(2):
        blocks = []
        for first in range(SIDE):
            block = tiles[first][0, 0, part]
            live = rank_table[place[6], tile_at(place, -first, -second)]
            index = lax.broadcasted_iota(jnp.int32, block.shape, 0)
            blocks.append(jnp.where(index < live, block, jnp.zeros_like(block)))
        turned = jnp.concatenate(blocks, axis=0).T
        high[part], low[part] = split(turned)


def receiver_bases(place, rank_table, u_bases):
    _, _, parts, ranks, receivers = u_bases.shape
    tile_spec = lambda first: pl.BlockSpec(
        (1, 1, parts, ranks, receivers),
        lambda second, place, table: (0, tile_at(place, -first, -second), 0, 0, 0),
    )
    shape = jax.ShapeDtypeStruct((parts, receivers, SIDE * SIDE * ranks), jnp.bfloat16)
    out_spec = pl.BlockSpec(
        (parts, receivers, SIDE * ranks), lambda second, place, table: (0, 0, second)
    )
    return call(
        bases_kernel,
        "receiver_bases",
        [shape] * 2,
        moved=12 << 20,
        grid_spec=pltpu.PrefetchScalarGridSpec(
            num_scalar_prefetch=2,
            grid=(SIDE,),
            in_specs=[tile_spec(first) for first in range(SIDE)],
            out_specs=[out_spec] * 2,
        ),
    )(place, rank_table, *[u_bases] * SIDE)


def field_kernel(place, *refs):
    arrived = refs[:SIDE]
    base_high, base_low, keep, send, right_high, right_low = refs[SIDE:]
    step = pl.program_id(0)

    @pl.when(step == 0)
    def _():
        for second in range(SIDE):
            block = arrived[second][...]
            rows = block.shape[0] * block.shape[1]
            high, low = split(block.reshape(rows, block.shape[2]))
            right_high[second * rows : (second + 1) * rows] = high
            right_low[second * rows : (second + 1) * rows] = low

    parts, receivers, depth = base_high.shape
    left = (
        base_high[...].reshape(parts * receivers, depth),
        base_low[...].reshape(parts * receivers, depth),
    )
    product = dot_split(left, (right_high[...], right_low[...]))
    width = product.shape[1] // 2
    upper, lower = product[:receivers], product[receivers:]
    real = upper[:, :width] - lower[:, width:]
    imag = upper[:, width:] + lower[:, :width]
    share = keep.shape[2]
    own = place[4] == 0
    for local in range(receivers // (2 * share)):
        slot = (step * (receivers // (2 * share)) + local - place[5]) & (RING - 1)
        for part, value in enumerate((real, imag)):
            even = value[2 * share * local : 2 * share * local + share]
            odd = value[2 * share * local + share : 2 * share * (local + 1)]
            keep[slot, part] = jnp.where(own, even, odd)
            send[slot, part] = jnp.where(own, odd, even)


def field(place, arrived, bases):
    parts, receivers, depth = bases[0].shape
    columns = arrived[0].shape[2]
    share = receivers // (2 * RING)
    steps = 2
    shape = (RING, 2, share, columns // 2)
    return call(
        field_kernel,
        f"field_{columns // 2}",
        [jax.ShapeDtypeStruct(shape, jnp.float32)] * 2,
        flops=2 * 3 * parts * receivers * depth * columns,
        moved=9 << 20,
        grid_spec=pltpu.PrefetchScalarGridSpec(
            num_scalar_prefetch=1,
            grid=(steps,),
            in_specs=[pl.BlockSpec(arrived[0].shape, lambda i, place: (0, 0, 0))] * SIDE
            + [pl.BlockSpec((parts, receivers // steps, depth), lambda i, place: (0, i, 0))] * 2,
            out_specs=[pl.BlockSpec(shape, lambda i, place: (0, 0, 0, 0))] * 2,
            scratch_shapes=[pltpu.VMEM((depth, columns), jnp.bfloat16)] * 2,
        ),
    )(place, *arrived, *bases)


def regroup_kernel(keep, got, *outs):
    for step, out in enumerate(outs):
        out[0] = keep[step]
        out[1] = got[step]


def regroup(keep, got):
    shape = (2,) + keep.shape[1:]
    whole = pl.BlockSpec(keep.shape, lambda i: (0, 0, 0, 0))
    return call(
        regroup_kernel,
        "regroup",
        [jax.ShapeDtypeStruct(shape, jnp.float32)] * RING,
        grid=(1,),
        in_specs=[whole] * 2,
        out_specs=[pl.BlockSpec(shape, lambda i: (0, 0, 0, 0))] * RING,
    )(keep, got)


def mute_tables(freq_count):
    sample = np.arange(PERIOD)[:, None]
    cycle = FLOW // FSTEP + np.arange(freq_count)[None, :]
    angles = (sample * cycle % PERIOD) * (2.0 * math.pi / PERIOD)
    forward = np.stack([np.cos(angles), -np.sin(angles)], axis=2)
    spread = np.kron(forward.reshape(PERIOD, 2 * freq_count), np.eye(GROUP)).astype(np.float32)
    tables = []
    for table in (spread * np.float32(2.0 / NT), spread.T):
        high = table.astype(jnp.bfloat16)
        low = (table - high.astype(np.float32)).astype(jnp.bfloat16)
        tables += [jnp.asarray(high), jnp.asarray(low)]
    return tables


def mute_kernel(place, *refs):
    pieces = refs[:RING]
    mute, inv_high, inv_low, fwd_high, fwd_low = refs[RING : RING + 5]
    out, gathered = refs[-2:]
    for step in range(RING):
        ring = (place[5] - step) & (RING - 1)
        for other in range(2):
            index = 2 * ring + (place[4] ^ other)
            for group in range(2):
                gathered[group, index] = pieces[step][other, :, GROUP * group : GROUP * (group + 1)]
    rows = inv_high.shape[1]
    right = jnp.concatenate([gathered[group].reshape(rows, LANES) for group in range(2)], axis=1)
    trace = dot_split((inv_high[...], inv_low[...]), split(right))
    trace = trace.reshape(PERIOD, GROUP, 2 * LANES)
    limit = jnp.concatenate([mute[:GROUP], mute[GROUP:]], axis=1)
    sample = lax.broadcasted_iota(jnp.int32, trace.shape, 0)
    count = (limit[None] - sample + (PERIOD - 1)) >> (PERIOD.bit_length() - 1)
    live = (trace * count.astype(jnp.float32)).reshape(PERIOD * GROUP, 2 * LANES)
    result = dot_split((fwd_high[...], fwd_low[...]), split(live))
    for group in range(2):
        part = result[:, LANES * group : LANES * (group + 1)]
        out[:, :, GROUP * group : GROUP * (group + 1)] = part.reshape(-1, 2, GROUP, LANES)


def time_mute(place, pieces, mute_rows, tables, start, before):
    _, parts, receivers, width = pieces[0].shape
    points = mute_rows.shape[1]
    freqs = 2 * RING
    offset = start // LANES
    whole = lambda shape: pl.BlockSpec(shape, lambda j, h, place: (0, 0))
    in_specs = [pl.BlockSpec((2, parts, 2 * GROUP, LANES), lambda j, h, place: (0, 0, h, j))] * RING
    in_specs += [pl.BlockSpec((2 * GROUP, LANES), lambda j, h, place: (h, offset + j))]
    in_specs += [whole(table.shape) for table in tables]
    operands = [place, *pieces, mute_rows, *tables]
    aliases = {}
    if before is not None:
        aliases = {len(operands): 0}
        in_specs += [pl.BlockSpec(memory_space=pl.ANY)]
        operands += [before]
    return call(
        mute_kernel,
        f"time_mute_{start}",
        jax.ShapeDtypeStruct((freqs, parts, receivers, points), jnp.float32),
        flops=2 * 6 * tables[0].size * (receivers // GROUP) * width,
        moved=4 << 20,
        grid_spec=pltpu.PrefetchScalarGridSpec(
            num_scalar_prefetch=1,
            grid=(width // LANES, receivers // (2 * GROUP)),
            in_specs=in_specs,
            out_specs=pl.BlockSpec(
                (freqs, parts, 2 * GROUP, LANES), lambda j, h, place: (0, 0, h, offset + j)
            ),
            scratch_shapes=[pltpu.VMEM((2, freqs, parts, GROUP, LANES), jnp.float32)],
        ),
        input_output_aliases=aliases,
    )(*operands)


def body(x_in, v_bases, u_bases, ranks, mute):
    place = place_of_device()
    rank_count = v_bases.shape[3]
    v_bases = jnp.swapaxes(v_bases, 3, 4)
    order = (2, 1, 3)
    packed = {first: pack(place, v_bases, x_in, first) for first in order + (0,)}
    near = {0: packed[0]}
    for first in order:
        near[first] = plane_shift(packed[first], first, 0)
    rest = x_in[0, :, :, WIDTHS[0] :]
    rests = {0: rest}
    for first in order:
        rests[first] = plane_shift(rest, first, 0)
    bases = receiver_bases(place, ranks[0], u_bases)
    tables = mute_tables(2 * RING)
    inputs = [near[first] for first in range(SIDE)]
    waves = [rests[first] for first in range(SIDE)]
    result = None
    start = 0
    for width in WIDTHS:
        if start == 0:
            blocks = coefficients(inputs, [], rank_count, 0, width)
        else:
            blocks = coefficients(inputs, waves, rank_count, start - WIDTHS[0], width)
        arrived = {0: blocks[0]}
        for second in order:
            arrived[second] = plane_shift(blocks[second], 0, second)
        keep, send = field(place, [arrived[second] for second in range(SIDE)], bases)
        pieces = regroup(keep, ring_shift(send, 0, 1))
        landed = {0: pieces[0]}
        for step in (4, 3, 5, 2, 6, 1, 7):
            landed[step] = ring_shift(pieces[step], step, 0)
        result = time_mute(
            place, [landed[step] for step in range(RING)], mute[0], tables, start, result
        )
        start += width
    return result[None]


def solution(mesh):
    placed = (
        P("freq", None, "tile", None),
        P("freq", None, None, None, "tile"),
        P("freq", None, None, None, "tile"),
        P("freq", None, None),
        P("tile", "freq", None),
    )
    return jax.shard_map(
        body,
        mesh=mesh,
        in_specs=placed,
        out_specs=P("tile", None, None, "freq", None),
        check_vma=False,
    )
```

```python
import functools
import math

import jax
import jax.numpy as jnp
import numpy as np
from jax import lax
from jax.experimental import pallas as pl
from jax.experimental.pallas import tpu as pltpu
from jax.sharding import PartitionSpec as P


NT = 512
FLOW = 20
FSTEP = 4
PERIOD = NT // FSTEP
GROUP = 8
SIDE = 4
RING = 8
LANES = 128
WIDTHS = (256, 256)
RING_ORDER = (4, 3, 5, 2, 6, 1, 7)


def split(value):
    high = value.astype(jnp.bfloat16)
    low = (value - high.astype(jnp.float32)).astype(jnp.bfloat16)
    return high, low


def dot(left, right):
    return jnp.dot(left, right, preferred_element_type=jnp.float32)


def dot_split(left, right):
    return dot(left[0], right[0]) + (dot(left[0], right[1]) + dot(left[1], right[0]))


def call(kernel, out_shape, flops=0, moved=1 << 20, limit=18, **kwargs):
    return pl.pallas_call(
        kernel,
        out_shape=out_shape,
        compiler_params=pltpu.CompilerParams(vmem_limit_bytes=limit << 20),
        cost_estimate=pl.CostEstimate(flops=flops, bytes_accessed=moved, transcendentals=0),
        **kwargs,
    )


def place_of_device():
    tile = lax.axis_index("tile")
    freq = lax.axis_index("freq")
    core = freq % 2
    straight = core == 0
    high, low = tile // SIDE, tile % SIDE
    values = (
        jnp.where(straight, high, low),
        jnp.where(straight, low, high),
        jnp.where(straight, SIDE, 1),
        jnp.where(straight, 1, SIDE),
        core,
        freq // 2,
        tile,
    )
    slot = lax.broadcasted_iota(jnp.int32, (8,), 0)
    place = jnp.zeros((8,), jnp.int32)
    for index, value in enumerate(values):
        place = jnp.where(slot == index, value.astype(jnp.int32), place)
    return place


def tile_at(place, first, second):
    return ((place[0] + first) & (SIDE - 1)) * place[2] + ((place[1] + second) & (SIDE - 1)) * place[3]


def plane_shift(array, first, second):
    pairs = []
    for freq in range(2 * RING):
        strides = (SIDE, 1) if freq % 2 == 0 else (1, SIDE)
        for one in range(SIDE):
            for two in range(SIDE):
                source = one * strides[0] + two * strides[1]
                target = (one + first) % SIDE * strides[0] + (two + second) % SIDE * strides[1]
                pairs.append((freq * SIDE * SIDE + source, freq * SIDE * SIDE + target))
    return lax.ppermute(array, ("freq", "tile"), pairs)


def ring_shift(array, step, swap):
    pairs = [
        (z * 2 + core, (z + step) % RING * 2 + (core + swap) % 2)
        for z in range(RING)
        for core in range(2)
    ]
    return lax.ppermute(array, "freq", pairs)


def pack_kernel(place, *refs):
    tiles, x_ref, out = refs[:SIDE], refs[SIDE], refs[SIDE + 1]
    ranks = tiles[0].shape[4]
    blocks = [tile[0, 0, part].T for tile in tiles for part in range(2)]
    out[:ranks] = jnp.concatenate(blocks, axis=1)
    span = out.shape[1] // SIDE
    rows = span * LANES // out.shape[1]
    wave = x_ref[0].reshape(span, -1)
    for column in range(wave.shape[1] // LANES):
        part = wave[:, LANES * column : LANES * (column + 1)]
        pieces = [part[start : start + rows] for start in range(0, span, rows)]
        base = ranks + rows * column
        out[base : base + rows] = jnp.concatenate(pieces, axis=1)


def pack(place, v_bases, x_in, first):
    _, _, parts, sources, ranks = v_bases.shape
    width = SIDE * parts * sources
    rows = ranks + parts * sources * WIDTHS[0] // width
    tile_spec = lambda second: pl.BlockSpec(
        (1, 1, parts, sources, ranks), lambda i, place: (0, tile_at(place, first, second), 0, 0, 0)
    )
    return call(
        pack_kernel,
        jax.ShapeDtypeStruct((rows, width), jnp.float32),
        grid_spec=pltpu.PrefetchScalarGridSpec(
            num_scalar_prefetch=1,
            grid=(1,),
            in_specs=[tile_spec(second) for second in range(SIDE)]
            + [pl.BlockSpec((1, parts, sources, WIDTHS[0]), lambda i, place: (0, 0, 0, 0))],
            out_specs=pl.BlockSpec((rows, width), lambda i, place: (0, 0)),
        ),
    )(place, *[v_bases] * SIDE, x_in)


def coefficient_kernel(ranks, *refs):
    packed = refs[:SIDE]
    waves = refs[SIDE:-SIDE]
    outs = refs[-SIDE:]
    for first in range(SIDE):
        rows = packed[first][...]
        span = rows.shape[1] // SIDE
        if waves:
            wave = waves[first][...].reshape(span, -1)
        else:
            height = span * LANES // rows.shape[1]
            columns = []
            for base in range(ranks, rows.shape[0], height):
                tail = rows[base : base + height]
                pieces = [tail[:, at : at + LANES] for at in range(0, rows.shape[1], LANES)]
                columns.append(jnp.concatenate(pieces, axis=0))
            wave = jnp.concatenate(columns, axis=1)
        real, imag = wave[: span // 2], wave[span // 2 :]
        right = jnp.concatenate(
            [jnp.concatenate([real, imag], axis=1), jnp.concatenate([imag, -real], axis=1)], axis=0
        )
        left = jnp.concatenate(
            [rows[:ranks, span * second : span * (second + 1)] for second in range(SIDE)], axis=0
        )
        result = dot_split(split(left), split(right))
        for second in range(SIDE):
            outs[second][first] = result[ranks * second : ranks * (second + 1)]


def coefficients(packed, waves, ranks, start, width):
    rows, span = packed[0].shape
    sources = span // SIDE
    in_specs = [pl.BlockSpec((rows, span), lambda i: (0, 0))] * SIDE
    if waves:
        block = start // width
        in_specs += [pl.BlockSpec((2, sources // 2, width), lambda i: (0, 0, block))] * SIDE
    shape = (SIDE, ranks, 2 * width)
    return call(
        functools.partial(coefficient_kernel, ranks),
        [jax.ShapeDtypeStruct(shape, jnp.float32)] * SIDE,
        flops=2 * 3 * SIDE * SIDE * ranks * sources * 2 * width,
        moved=4 << 20,
        grid=(1,),
        in_specs=in_specs,
        out_specs=[pl.BlockSpec(shape, lambda i: (0, 0, 0))] * SIDE,
    )(*packed, *waves)


def bases_kernel(place, rank_table, *refs):
    tiles, high, low = refs[:SIDE], refs[SIDE], refs[SIDE + 1]
    second = pl.program_id(0)
    for part in range(2):
        blocks = []
        for first in range(SIDE):
            block = tiles[first][0, 0, part]
            live = rank_table[place[6], tile_at(place, -first, -second)]
            index = lax.broadcasted_iota(jnp.int32, block.shape, 0)
            blocks.append(jnp.where(index < live, block, jnp.zeros_like(block)))
        turned = jnp.concatenate(blocks, axis=0).T
        high[part], low[part] = split(turned)


def receiver_bases(place, rank_table, u_bases):
    _, _, parts, ranks, receivers = u_bases.shape
    tile_spec = lambda first: pl.BlockSpec(
        (1, 1, parts, ranks, receivers),
        lambda second, place, table: (0, tile_at(place, -first, -second), 0, 0, 0),
    )
    shape = jax.ShapeDtypeStruct((parts, receivers, SIDE * SIDE * ranks), jnp.bfloat16)
    out_spec = pl.BlockSpec(
        (parts, receivers, SIDE * ranks), lambda second, place, table: (0, 0, second)
    )
    return call(
        bases_kernel,
        [shape] * 2,
        moved=12 << 20,
        grid_spec=pltpu.PrefetchScalarGridSpec(
            num_scalar_prefetch=2,
            grid=(SIDE,),
            in_specs=[tile_spec(first) for first in range(SIDE)],
            out_specs=[out_spec] * 2,
        ),
    )(place, rank_table, *[u_bases] * SIDE)


def field_kernel(place, *refs):
    arrived = refs[:SIDE]
    base_high, base_low, keep, send, right_high, right_low = refs[SIDE:]
    step = pl.program_id(0)

    @pl.when(step == 0)
    def _():
        for second in range(SIDE):
            block = arrived[second][...]
            rows = block.shape[0] * block.shape[1]
            high, low = split(block.reshape(rows, block.shape[2]))
            right_high[second * rows : (second + 1) * rows] = high
            right_low[second * rows : (second + 1) * rows] = low

    parts, receivers, depth = base_high.shape
    left = (
        base_high[...].reshape(parts * receivers, depth),
        base_low[...].reshape(parts * receivers, depth),
    )
    product = dot_split(left, (right_high[...], right_low[...]))
    width = product.shape[1] // 2
    upper, lower = product[:receivers], product[receivers:]
    real = upper[:, :width] - lower[:, width:]
    imag = upper[:, width:] + lower[:, :width]
    share = keep.shape[2]
    own = place[4] == 0
    for local in range(receivers // (2 * share)):
        slot = (step * (receivers // (2 * share)) + local - place[5]) & (RING - 1)
        for part, value in enumerate((real, imag)):
            even = value[2 * share * local : 2 * share * local + share]
            odd = value[2 * share * local + share : 2 * share * (local + 1)]
            keep[slot, part] = jnp.where(own, even, odd)
            send[slot, part] = jnp.where(own, odd, even)


def field(place, arrived, bases):
    parts, receivers, depth = bases[0].shape
    columns = arrived[0].shape[2]
    share = receivers // (2 * RING)
    steps = 4
    shape = (RING, 2, share, columns // 2)
    return call(
        field_kernel,
        [jax.ShapeDtypeStruct(shape, jnp.float32)] * 2,
        flops=2 * 3 * parts * receivers * depth * columns,
        moved=9 << 20,
        grid_spec=pltpu.PrefetchScalarGridSpec(
            num_scalar_prefetch=1,
            grid=(steps,),
            in_specs=[pl.BlockSpec(arrived[0].shape, lambda i, place: (0, 0, 0))] * SIDE
            + [pl.BlockSpec((parts, receivers // steps, depth), lambda i, place: (0, i, 0))] * 2,
            out_specs=[pl.BlockSpec(shape, lambda i, place: (0, 0, 0, 0))] * 2,
            scratch_shapes=[pltpu.VMEM((depth, columns), jnp.bfloat16)] * 2,
        ),
    )(place, *arrived, *bases)


def regroup_kernel(keep, got, *outs):
    for step, out in enumerate(outs):
        out[0] = keep[step]
        out[1] = got[step]


def regroup(keep, got):
    shape = (2,) + keep.shape[1:]
    whole = pl.BlockSpec(keep.shape, lambda i: (0, 0, 0, 0))
    return call(
        regroup_kernel,
        [jax.ShapeDtypeStruct(shape, jnp.float32)] * RING,
        grid=(1,),
        in_specs=[whole] * 2,
        out_specs=[pl.BlockSpec(shape, lambda i: (0, 0, 0, 0))] * RING,
    )(keep, got)


def table_kernel(high, low, high_turned, low_turned, inverse, forward):
    block = forward.shape[1]

    def spread(table):
        rows, columns = table.shape
        shape = (columns, GROUP * columns)
        chosen = lax.broadcasted_iota(jnp.int32, shape, 0) == lax.broadcasted_iota(
            jnp.int32, shape, 1
        ) // GROUP
        wide = dot(table, chosen.astype(jnp.float32).astype(jnp.bfloat16))
        wide = jnp.broadcast_to(wide[:, None], (rows, GROUP, GROUP * columns))
        wide = wide.reshape(rows * GROUP, GROUP * columns)
        row = lax.broadcasted_iota(jnp.int32, wide.shape, 0)
        column = lax.broadcasted_iota(jnp.int32, wide.shape, 1)
        return jnp.where((row & (GROUP - 1)) == (column & (GROUP - 1)), wide, 0.0)

    first = (spread(high[...]) * (2.0 / NT)).astype(jnp.bfloat16)
    second = (spread(low[...]) * (2.0 / NT)).astype(jnp.bfloat16)
    inverse[...] = jnp.concatenate([first, second, first], axis=1)
    first = spread(high_turned[...]).astype(jnp.bfloat16)
    second = spread(low_turned[...]).astype(jnp.bfloat16)
    for index in range(forward.shape[0]):
        at = slice(block * index, block * (index + 1))
        forward[index] = jnp.concatenate([first[:, at], second[:, at], first[:, at]], axis=1)


def mute_tables(freq_count):
    sample = np.arange(PERIOD)[:, None]
    cycle = FLOW // FSTEP + np.arange(freq_count)[None, :]
    angles = (sample * cycle % PERIOD) * (2.0 * math.pi / PERIOD)
    table = np.stack([np.cos(angles), -np.sin(angles)], axis=2)
    table = table.reshape(PERIOD, 2 * freq_count).astype(np.float32)
    high = table.astype(jnp.bfloat16)
    low = (table - high.astype(np.float32)).astype(jnp.bfloat16)
    parts = [jnp.asarray(part) for part in (high, low, high.T.copy(), low.T.copy())]
    block = 2 * freq_count * GROUP
    shapes = ((PERIOD * GROUP, 3 * block), (PERIOD * GROUP // block, block, 3 * block))
    return call(
        table_kernel, [jax.ShapeDtypeStruct(shape, jnp.bfloat16) for shape in shapes], moved=3 << 20
    )(*parts)


def mute_kernel(place, *refs):
    pieces = refs[:RING]
    mute, inverse, forward = refs[RING : RING + 3]
    out, gathered = refs[-2:]
    for step in range(RING):
        ring = (place[5] - step) & (RING - 1)
        for other in range(2):
            index = 2 * ring + (place[4] ^ other)
            for group in range(2):
                gathered[group, index] = pieces[step][other, :, GROUP * group : GROUP * (group + 1)]
    blocks, rows, _ = forward.shape
    samples = rows // GROUP
    limit = jnp.concatenate([mute[:GROUP], mute[GROUP:]], axis=1)

    def stacked(value):
        high, low = split(value)
        return jnp.concatenate([high, high, low], axis=0)

    right = stacked(
        jnp.concatenate([gathered[group].reshape(rows, LANES) for group in range(2)], axis=1)
    )
    result = None
    for block in range(blocks):
        trace = dot(inverse[rows * block : rows * (block + 1)], right)
        trace = trace.reshape(samples, GROUP, 2 * LANES)
        sample = lax.broadcasted_iota(jnp.int32, trace.shape, 0) + samples * block
        count = (limit[None] - sample + (PERIOD - 1)) >> (PERIOD.bit_length() - 1)
        live = (trace * count.astype(jnp.float32)).reshape(rows, 2 * LANES)
        term = dot(forward[block], stacked(live))
        result = term if result is None else result + term
    for group in range(2):
        part = result[:, LANES * group : LANES * (group + 1)]
        out[:, :, GROUP * group : GROUP * (group + 1)] = part.reshape(-1, 2, GROUP, LANES)


def time_mute(place, pieces, mute_rows, tables, start, before):
    _, parts, receivers, width = pieces[0].shape
    points = mute_rows.shape[1]
    freqs = 2 * RING
    offset = start // LANES
    whole = lambda shape: pl.BlockSpec(shape, lambda j, h, place: (0,) * len(shape))
    in_specs = [pl.BlockSpec((2, parts, 2 * GROUP, LANES), lambda j, h, place: (0, 0, h, j))] * RING
    in_specs += [pl.BlockSpec((2 * GROUP, LANES), lambda j, h, place: (h, offset + j))]
    in_specs += [whole(table.shape) for table in tables]
    operands = [place, *pieces, mute_rows, *tables]
    aliases = {}
    if before is not None:
        aliases = {len(operands): 0}
        in_specs += [pl.BlockSpec(memory_space=pl.ANY)]
        operands += [before]
    return call(
        mute_kernel,
        jax.ShapeDtypeStruct((freqs, parts, receivers, points), jnp.float32),
        flops=2 * 2 * tables[0].size * (receivers // GROUP) * width,
        moved=4 << 20,
        grid_spec=pltpu.PrefetchScalarGridSpec(
            num_scalar_prefetch=1,
            grid=(width // LANES, receivers // (2 * GROUP)),
            in_specs=in_specs,
            out_specs=pl.BlockSpec(
                (freqs, parts, 2 * GROUP, LANES), lambda j, h, place: (0, 0, h, offset + j)
            ),
            scratch_shapes=[pltpu.VMEM((2, freqs, parts, GROUP, LANES), jnp.float32)],
        ),
        input_output_aliases=aliases,
    )(*operands)


def step(x_in, v_bases, u_bases, ranks, mute):
    place = place_of_device()
    rank_count = v_bases.shape[3]
    v_bases = jnp.swapaxes(v_bases, 3, 4)
    order = (2, 1, 3)
    packed = {first: pack(place, v_bases, x_in, first) for first in order + (0,)}
    near = {0: packed[0]}
    for first in order:
        near[first] = plane_shift(packed[first], first, 0)
    rest = x_in[0, :, :, WIDTHS[0] :]
    rests = {0: rest}
    for first in order:
        rests[first] = plane_shift(rest, first, 0)
    bases = receiver_bases(place, ranks[0], u_bases)
    tables = mute_tables(2 * RING)
    inputs = [near[first] for first in range(SIDE)]
    waves = [rests[first] for first in range(SIDE)]
    result = None
    start = 0
    for width in WIDTHS:
        if start == 0:
            blocks = coefficients(inputs, [], rank_count, 0, width)
        else:
            blocks = coefficients(inputs, waves, rank_count, start - WIDTHS[0], width)
        arrived = {0: blocks[0]}
        for second in order:
            arrived[second] = plane_shift(blocks[second], 0, second)
        keep, send = field(place, [arrived[second] for second in range(SIDE)], bases)
        got = ring_shift(send, 0, 1)
        pieces = regroup(keep, got)
        landed = {0: pieces[0]}
        for turn in RING_ORDER:
            landed[turn] = ring_shift(pieces[turn], turn, 0)
        result = time_mute(
            place, [landed[turn] for turn in range(RING)], mute[0], tables, start, result
        )
        start += width
    return result[None]


def solution(mesh):
    placed = (
        P("freq", None, "tile", None),
        P("freq", None, None, None, "tile"),
        P("freq", None, None, None, "tile"),
        P("freq", None, None),
        P("tile", "freq", None),
    )
    return jax.shard_map(
        step,
        mesh=mesh,
        in_specs=placed,
        out_specs=P("tile", None, None, "freq", None),
        check_vma=False,
    )
```

```python
import functools
import math

import jax
import jax.numpy as jnp
import numpy as np
from jax import lax
from jax.experimental import pallas as pl
from jax.experimental.pallas import tpu as pltpu
from jax.sharding import PartitionSpec as P


NT = 512
FLOW = 20
FSTEP = 4
PERIOD = NT // FSTEP
HALF = PERIOD // 2
GROUP = 8
SIDE = 4
PACK_LIMIT = 18
RING = 8
LANES = 128
BATCHES = ((128, 128), (256,))
RING_ORDER = (4, 3, 5, 2, 6, 1, 7)
FIRST = sum(BATCHES[0])


def split(value):
    high = value.astype(jnp.bfloat16)
    low = (value - high.astype(jnp.float32)).astype(jnp.bfloat16)
    return high, low


def dot(left, right):
    return jnp.dot(left, right, preferred_element_type=jnp.float32)


def dot_split(left, right):
    return dot(left[0], right[0]) + (dot(left[0], right[1]) + dot(left[1], right[0]))


def call(kernel, out_shape, flops=0, moved=1 << 20, limit=18, **kwargs):
    return pl.pallas_call(
        kernel,
        out_shape=out_shape,
        compiler_params=pltpu.CompilerParams(vmem_limit_bytes=limit << 20),
        cost_estimate=pl.CostEstimate(flops=flops, bytes_accessed=moved, transcendentals=0),
        **kwargs,
    )


def place_of_device():
    tile = lax.axis_index("tile")
    freq = lax.axis_index("freq")
    core = freq % 2
    straight = core == 0
    high, low = tile // SIDE, tile % SIDE
    values = (
        jnp.where(straight, high, low),
        jnp.where(straight, low, high),
        jnp.where(straight, SIDE, 1),
        jnp.where(straight, 1, SIDE),
        core,
        freq // 2,
        tile,
    )
    slot = lax.broadcasted_iota(jnp.int32, (8,), 0)
    place = jnp.zeros((8,), jnp.int32)
    for index, value in enumerate(values):
        place = jnp.where(slot == index, value.astype(jnp.int32), place)
    return place


def tile_at(place, first, second):
    return ((place[0] + first) & (SIDE - 1)) * place[2] + ((place[1] + second) & (SIDE - 1)) * place[3]


def plane_shift(array, first, second):
    pairs = []
    for freq in range(2 * RING):
        strides = (SIDE, 1) if freq % 2 == 0 else (1, SIDE)
        for one in range(SIDE):
            for two in range(SIDE):
                source = one * strides[0] + two * strides[1]
                target = (one + first) % SIDE * strides[0] + (two + second) % SIDE * strides[1]
                pairs.append((freq * SIDE * SIDE + source, freq * SIDE * SIDE + target))
    return lax.ppermute(array, ("freq", "tile"), pairs)


def ring_shift(array, step, swap):
    pairs = [
        (z * 2 + core, (z + step) % RING * 2 + (core + swap) % 2)
        for z in range(RING)
        for core in range(2)
    ]
    return lax.ppermute(array, "freq", pairs)


def pack_kernel(place, *refs):
    tiles, x_ref, out = refs[:SIDE], refs[SIDE], refs[SIDE + 1]
    ranks = tiles[0].shape[4]
    blocks = [tile[0, 0, part].T for tile in tiles for part in range(2)]
    out[:ranks] = jnp.concatenate(blocks, axis=1)
    span = out.shape[1] // SIDE
    rows = span * LANES // out.shape[1]
    wave = x_ref[0].reshape(span, -1)
    for column in range(wave.shape[1] // LANES):
        part = wave[:, LANES * column : LANES * (column + 1)]
        pieces = [part[start : start + rows] for start in range(0, span, rows)]
        base = ranks + rows * column
        out[base : base + rows] = jnp.concatenate(pieces, axis=1)


def pack(place, v_bases, x_in, first):
    _, _, parts, sources, ranks = v_bases.shape
    width = SIDE * parts * sources
    rows = ranks + parts * sources * FIRST // width
    tile_spec = lambda second: pl.BlockSpec(
        (1, 1, parts, sources, ranks), lambda i, place: (0, tile_at(place, first, second), 0, 0, 0)
    )
    return call(
        pack_kernel,
        jax.ShapeDtypeStruct((rows, width), jnp.float32),
        limit=PACK_LIMIT,
        grid_spec=pltpu.PrefetchScalarGridSpec(
            num_scalar_prefetch=1,
            grid=(1,),
            in_specs=[tile_spec(second) for second in range(SIDE)]
            + [pl.BlockSpec((1, parts, sources, FIRST), lambda i, place: (0, 0, 0, 0))],
            out_specs=pl.BlockSpec((rows, width), lambda i, place: (0, 0)),
        ),
    )(place, *[v_bases] * SIDE, x_in)


def coefficient_kernel(ranks, start, width, *refs):
    packed = refs[:SIDE]
    waves = refs[SIDE:-SIDE]
    outs = refs[-SIDE:]
    for first in range(SIDE):
        rows = packed[first][...]
        span = rows.shape[1] // SIDE
        if waves:
            wave = waves[first][...].reshape(span, -1)
        else:
            height = span * LANES // rows.shape[1]
            columns = []
            begin = ranks + height * start // LANES
            for base in range(begin, begin + height * width // LANES, height):
                tail = rows[base : base + height]
                pieces = [tail[:, at : at + LANES] for at in range(0, rows.shape[1], LANES)]
                columns.append(jnp.concatenate(pieces, axis=0))
            wave = jnp.concatenate(columns, axis=1)
        real, imag = wave[: span // 2], wave[span // 2 :]
        right = jnp.concatenate(
            [jnp.concatenate([real, imag], axis=1), jnp.concatenate([imag, -real], axis=1)], axis=0
        )
        left = jnp.concatenate(
            [rows[:ranks, span * second : span * (second + 1)] for second in range(SIDE)], axis=0
        )
        result = dot_split(split(left), split(right))
        for second in range(SIDE):
            outs[second][first] = result[ranks * second : ranks * (second + 1)]


def coefficients(packed, waves, ranks, start, width):
    rows, span = packed[0].shape
    sources = span // SIDE
    in_specs = [pl.BlockSpec((rows, span), lambda i: (0, 0))] * SIDE
    if waves:
        block = start // width
        in_specs += [pl.BlockSpec((2, sources // 2, width), lambda i: (0, 0, block))] * SIDE
    shape = (SIDE, ranks, 2 * width)
    return call(
        functools.partial(coefficient_kernel, ranks, start, width),
        [jax.ShapeDtypeStruct(shape, jnp.float32)] * SIDE,
        flops=2 * 3 * SIDE * SIDE * ranks * sources * 2 * width,
        moved=4 << 20,
        grid=(1,),
        in_specs=in_specs,
        out_specs=[pl.BlockSpec(shape, lambda i: (0, 0, 0))] * SIDE,
    )(*packed, *waves)


def bases_kernel(place, rank_table, *refs):
    tiles, out = refs[:SIDE], refs[SIDE]
    second = pl.program_id(0)
    for part in range(2):
        blocks = []
        for first in range(SIDE):
            block = tiles[first][0, 0, part]
            live = rank_table[place[6], tile_at(place, -first, -second)]
            index = lax.broadcasted_iota(jnp.int32, block.shape, 0)
            blocks.append(jnp.where(index < live, block, jnp.zeros_like(block)))
        turned = jnp.concatenate(blocks, axis=0).T
        out[0, part], out[1, part] = split(turned)


def receiver_bases(place, rank_table, u_bases):
    _, _, parts, ranks, receivers = u_bases.shape
    tile_spec = lambda first: pl.BlockSpec(
        (1, 1, parts, ranks, receivers),
        lambda second, place, table: (0, tile_at(place, -first, -second), 0, 0, 0),
    )
    shape = jax.ShapeDtypeStruct((2, parts, receivers, SIDE * SIDE * ranks), jnp.bfloat16)
    out_spec = pl.BlockSpec(
        (2, parts, receivers, SIDE * ranks), lambda second, place, table: (0, 0, 0, second)
    )
    return call(
        bases_kernel,
        shape,
        moved=12 << 20,
        grid_spec=pltpu.PrefetchScalarGridSpec(
            num_scalar_prefetch=2,
            grid=(SIDE,),
            in_specs=[tile_spec(first) for first in range(SIDE)],
            out_specs=out_spec,
        ),
    )(place, rank_table, *[u_bases] * SIDE)


def field_kernel(place, *refs):
    arrived = refs[:SIDE]
    bases, keep, send, right_high, right_low = refs[SIDE:]
    step = pl.program_id(0)

    @pl.when(step == 0)
    def _():
        for second in range(SIDE):
            block = arrived[second][...]
            rows = block.shape[0] * block.shape[1]
            high, low = split(block.reshape(rows, block.shape[2]))
            right_high[second * rows : (second + 1) * rows] = high
            right_low[second * rows : (second + 1) * rows] = low

    _, parts, receivers, depth = bases.shape
    rows = parts * receivers
    left = bases[...].reshape(2 * rows, depth)
    product = dot(left, right_high[...])
    product = product[:rows] + (product[rows:] + dot(left[:rows], right_low[...]))
    width = product.shape[1] // 2
    upper, lower = product[:receivers], product[receivers:]
    real = upper[:, :width] - lower[:, width:]
    imag = upper[:, width:] + lower[:, :width]
    share = keep.shape[2]
    own = place[4] == 0
    for local in range(receivers // (2 * share)):
        slot = (step * (receivers // (2 * share)) + local - place[5]) & (RING - 1)
        for part, value in enumerate((real, imag)):
            even = value[2 * share * local : 2 * share * local + share]
            odd = value[2 * share * local + share : 2 * share * (local + 1)]
            keep[slot, part] = jnp.where(own, even, odd)
            send[slot, part] = jnp.where(own, odd, even)


def field(place, arrived, bases):
    _, parts, receivers, depth = bases.shape
    columns = arrived[0].shape[2]
    share = receivers // (2 * RING)
    steps = 1
    shape = (RING, 2, share, columns // 2)
    return call(
        field_kernel,
        [jax.ShapeDtypeStruct(shape, jnp.float32)] * 2,
        flops=2 * 3 * parts * receivers * depth * columns,
        moved=9 << 20,
        grid_spec=pltpu.PrefetchScalarGridSpec(
            num_scalar_prefetch=1,
            grid=(steps,),
            in_specs=[pl.BlockSpec(arrived[0].shape, lambda i, place: (0, 0, 0))] * SIDE
            + [pl.BlockSpec((2, parts, receivers // steps, depth), lambda i, place: (0, 0, i, 0))],
            out_specs=[pl.BlockSpec(shape, lambda i, place: (0, 0, 0, 0))] * 2,
            scratch_shapes=[pltpu.VMEM((depth, columns), jnp.bfloat16)] * 2,
        ),
    )(place, *arrived, bases)


def regroup_kernel(*refs):
    fields, outs = refs[:-RING], refs[-RING:]
    for turn, out in enumerate(outs):
        start = 0
        for index in range(0, len(fields), 2):
            width = fields[index].shape[3]
            for other in range(2):
                out[other, :, :, start : start + width] = fields[index + other][turn]
            start += width


def regroup(fields):
    width = sum(array.shape[3] for array in fields) // 2
    shape = (2,) + fields[0].shape[1:3] + (width,)
    return call(
        regroup_kernel,
        [jax.ShapeDtypeStruct(shape, jnp.float32)] * RING,
        grid=(1,),
        in_specs=[pl.BlockSpec(array.shape, lambda i: (0, 0, 0, 0)) for array in fields],
        out_specs=[pl.BlockSpec(shape, lambda i: (0, 0, 0, 0))] * RING,
    )(*fields)


def spread(table):
    rows, columns = table.shape
    shape = (columns, GROUP * columns)
    index = lax.broadcasted_iota(jnp.int32, shape, 1) // GROUP
    chosen = lax.broadcasted_iota(jnp.int32, shape, 0) == index
    wide = dot(table, chosen.astype(jnp.float32).astype(jnp.bfloat16))
    wide = jnp.broadcast_to(wide[:, None], (rows, GROUP, GROUP * columns))
    wide = wide.reshape(rows * GROUP, GROUP * columns)
    row = lax.broadcasted_iota(jnp.int32, wide.shape, 0)
    column = lax.broadcasted_iota(jnp.int32, wide.shape, 1)
    return jnp.where((row & (GROUP - 1)) == (column & (GROUP - 1)), wide, 0.0)


def table_kernel(high, low, high_turned, low_turned, inverse, forward):
    for parity in range(2):
        first = (spread(high[parity]) * (2.0 / NT)).astype(jnp.bfloat16)
        second = (spread(low[parity]) * (2.0 / NT)).astype(jnp.bfloat16)
        inverse[parity] = jnp.concatenate([first, second, first], axis=1)
        first = spread(high_turned[parity]).astype(jnp.bfloat16)
        second = spread(low_turned[parity]).astype(jnp.bfloat16)
        block = forward.shape[3] // 3
        for index in range(forward.shape[1]):
            at = slice(block * index, block * (index + 1))
            pieces = [first[:, at], second[:, at], first[:, at]]
            forward[parity, index] = jnp.concatenate(pieces, axis=1)


def mute_tables(freq_count):
    sample = np.arange(HALF)[:, None]
    cycle = FLOW // FSTEP + np.arange(freq_count)[None, :]
    angles = (sample * cycle % PERIOD) * (2.0 * math.pi / PERIOD)
    table = np.stack([np.cos(angles), -np.sin(angles)], axis=2)
    table = table.reshape(HALF, freq_count // 2, 2, 2).transpose(2, 0, 1, 3)
    table = table.reshape(2, HALF, freq_count).astype(np.float32)
    high = table.astype(jnp.bfloat16)
    low = (table - high.astype(np.float32)).astype(jnp.bfloat16)
    turn = lambda array: np.ascontiguousarray(array.transpose(0, 2, 1))
    parts = [jnp.asarray(part) for part in (high, low, turn(high), turn(low))]
    rows = freq_count * GROUP
    shapes = ((2, HALF * GROUP, 3 * rows), (2, 2, rows, 3 * HALF * GROUP // 2))
    return call(
        table_kernel, [jax.ShapeDtypeStruct(shape, jnp.bfloat16) for shape in shapes], moved=2 << 20
    )(*parts)


def mute_kernel(place, *refs):
    pieces = refs[:RING]
    mute, inverse, forward = refs[RING : RING + 3]
    out, gathered = refs[-2:]
    for step in range(RING):
        ring = (place[5] - step) & (RING - 1)
        for other in range(2):
            parity = place[4] ^ other
            for group in range(2):
                value = pieces[step][other, :, GROUP * group : GROUP * (group + 1)]
                gathered[group, parity, ring] = value
    _, blocks, rows, _ = forward.shape
    span = HALF * GROUP // blocks
    samples = HALF // blocks
    limit = jnp.concatenate([mute[:GROUP], mute[GROUP:]], axis=1)[None]

    def stacked(value):
        high, low = split(value)
        return jnp.concatenate([high, high, low], axis=0)

    def count(sample):
        live = (limit - sample + (PERIOD - 1)) >> (PERIOD.bit_length() - 1)
        return live.astype(jnp.float32)

    waves = []
    for parity in range(2):
        columns = [gathered[group, parity].reshape(rows, LANES) for group in range(2)]
        waves.append(dot(inverse[parity], stacked(jnp.concatenate(columns, axis=1))))
    results = [None, None]
    for block in range(blocks):
        shape = (samples, GROUP, 2 * LANES)
        even, odd = [wave[span * block : span * (block + 1)].reshape(shape) for wave in waves]
        sample = lax.broadcasted_iota(jnp.int32, shape, 0) + samples * block
        near = (odd + even) * count(sample)
        far = (odd - even) * count(sample + HALF)
        for parity, value in enumerate((near - far, near + far)):
            term = dot(forward[parity, block], stacked(value.reshape(span, 2 * LANES)))
            results[parity] = term if block == 0 else results[parity] + term
    for parity in range(2):
        for group in range(2):
            part = results[parity][:, LANES * group : LANES * (group + 1)]
            part = part.reshape(RING, 2, GROUP, LANES)
            for ring in range(RING):
                out[2 * ring + parity, :, GROUP * group : GROUP * (group + 1)] = part[ring]


def time_mute(place, pieces, mute_rows, tables, start, before):
    _, parts, receivers, width = pieces[0].shape
    points = mute_rows.shape[1]
    freqs = 2 * RING
    offset = start // LANES
    whole = lambda shape: pl.BlockSpec(shape, lambda j, h, place: (0,) * len(shape))
    in_specs = [pl.BlockSpec((2, parts, 2 * GROUP, LANES), lambda j, h, place: (0, 0, h, j))] * RING
    in_specs += [pl.BlockSpec((2 * GROUP, LANES), lambda j, h, place: (h, offset + j))]
    in_specs += [whole(table.shape) for table in tables]
    operands = [place, *pieces, mute_rows, *tables]
    aliases = {}
    if before is not None:
        aliases = {len(operands): 0}
        in_specs += [pl.BlockSpec(memory_space=pl.ANY)]
        operands += [before]
    return call(
        mute_kernel,
        jax.ShapeDtypeStruct((freqs, parts, receivers, points), jnp.float32),
        flops=2 * 2 * tables[0].size * (receivers // GROUP) * width,
        moved=4 << 20,
        grid_spec=pltpu.PrefetchScalarGridSpec(
            num_scalar_prefetch=1,
            grid=(width // LANES, receivers // (2 * GROUP)),
            in_specs=in_specs,
            out_specs=pl.BlockSpec(
                (freqs, parts, 2 * GROUP, LANES), lambda j, h, place: (0, 0, h, offset + j)
            ),
            scratch_shapes=[pltpu.VMEM((2, 2, RING, parts, GROUP, LANES), jnp.float32)],
        ),
        input_output_aliases=aliases,
    )(*operands)


def step(x_in, v_bases, u_bases, ranks, mute):
    place = place_of_device()
    rank_count = v_bases.shape[3]
    v_bases = jnp.swapaxes(v_bases, 3, 4)
    order = (2, 1, 3)
    packed = {first: pack(place, v_bases, x_in, first) for first in order + (0,)}
    near = {0: packed[0]}
    for first in order:
        near[first] = plane_shift(packed[first], first, 0)
    rest = x_in[0, :, :, FIRST:]
    rests = {0: rest}
    for first in order:
        rests[first] = plane_shift(rest, first, 0)
    bases = receiver_bases(place, ranks[0], u_bases)
    tables = mute_tables(2 * RING)
    inputs = [near[first] for first in range(SIDE)]
    waves = [rests[first] for first in range(SIDE)]
    result = None
    chunk = start = done = 0
    for batch, widths in enumerate(BATCHES):
        fields = []
        for width in widths:
            shown = waves if batch else []
            offset = start - FIRST if batch else start
            blocks = coefficients(inputs, shown, rank_count, offset, width)
            arrived = {0: blocks[0]}
            for second in order:
                arrived[second] = plane_shift(blocks[second], 0, second)
            keep, send = field(place, [arrived[second] for second in range(SIDE)], bases)
            fields += [keep, ring_shift(send, 0, 1)]
            chunk += 1
            start += width
        pieces = regroup(fields)
        landed = {0: pieces[0]}
        for turn in RING_ORDER:
            landed[turn] = ring_shift(pieces[turn], turn, 0)
        result = time_mute(
            place, [landed[turn] for turn in range(RING)], mute[0], tables, done, result
        )
        done = start
    return result[None]


def solution(mesh):
    placed = (
        P("freq", None, "tile", None),
        P("freq", None, None, None, "tile"),
        P("freq", None, None, None, "tile"),
        P("freq", None, None),
        P("tile", "freq", None),
    )
    return jax.shard_map(
        step,
        mesh=mesh,
        in_specs=placed,
        out_specs=P("tile", None, None, "freq", None),
        check_vma=False,
    )
```

```python
import functools
import math

import jax
import jax.numpy as jnp
import numpy as np
from jax import lax
from jax.experimental import pallas as pl
from jax.experimental.pallas import tpu as pltpu
from jax.sharding import PartitionSpec as P


NT = 512
FLOW = 20
FSTEP = 4
PERIOD = NT // FSTEP
HALF = PERIOD // 2
GROUP = 8
SIDE = 4
SIDE_ORDER = (1, 3, 2)
PACK_LIMIT = 18
RING = 8
LANES = 128
BATCHES = ((128, 128), (256,))
RING_ORDER = (1, 7, 4, 3, 5, 2, 6)
FIRST = sum(BATCHES[0])


def split(value):
    high = value.astype(jnp.bfloat16)
    low = (value - high.astype(jnp.float32)).astype(jnp.bfloat16)
    return high, low


def dot(left, right):
    return jnp.dot(left, right, preferred_element_type=jnp.float32)


def dot_split(left, right):
    return dot(left[0], right[0]) + (dot(left[0], right[1]) + dot(left[1], right[0]))


def call(kernel, out_shape, flops=0, moved=1 << 20, limit=18, **kwargs):
    return pl.pallas_call(
        kernel,
        out_shape=out_shape,
        compiler_params=pltpu.CompilerParams(vmem_limit_bytes=limit << 20),
        cost_estimate=pl.CostEstimate(flops=flops, bytes_accessed=moved, transcendentals=0),
        **kwargs,
    )


def place_of_device():
    tile = lax.axis_index("tile")
    freq = lax.axis_index("freq")
    core = freq % 2
    straight = core == 0
    high, low = tile // SIDE, tile % SIDE
    values = (
        jnp.where(straight, high, low),
        jnp.where(straight, low, high),
        jnp.where(straight, SIDE, 1),
        jnp.where(straight, 1, SIDE),
        core,
        freq // 2,
        tile,
    )
    slot = lax.broadcasted_iota(jnp.int32, (8,), 0)
    place = jnp.zeros((8,), jnp.int32)
    for index, value in enumerate(values):
        place = jnp.where(slot == index, value.astype(jnp.int32), place)
    return place


def tile_at(place, first, second):
    return ((place[0] + first) & (SIDE - 1)) * place[2] + ((place[1] + second) & (SIDE - 1)) * place[3]


def plane_shift(array, first, second):
    pairs = []
    for freq in range(2 * RING):
        strides = (SIDE, 1) if freq % 2 == 0 else (1, SIDE)
        for one in range(SIDE):
            for two in range(SIDE):
                source = one * strides[0] + two * strides[1]
                target = (one + first) % SIDE * strides[0] + (two + second) % SIDE * strides[1]
                pairs.append((freq * SIDE * SIDE + source, freq * SIDE * SIDE + target))
    return lax.ppermute(array, ("freq", "tile"), pairs)


def ring_shift(array, step, swap):
    pairs = [
        (z * 2 + core, (z + step) % RING * 2 + (core + swap) % 2)
        for z in range(RING)
        for core in range(2)
    ]
    return lax.ppermute(array, "freq", pairs)


def pack_kernel(place, *refs):
    tiles, x_ref, out = refs[:SIDE], refs[SIDE], refs[SIDE + 1]
    ranks = tiles[0].shape[4]
    blocks = [tile[0, 0, part].T for tile in tiles for part in range(2)]
    out[:ranks] = jnp.concatenate(blocks, axis=1)
    span = out.shape[1] // SIDE
    rows = span * LANES // out.shape[1]
    wave = x_ref[0].reshape(span, -1)
    for column in range(wave.shape[1] // LANES):
        part = wave[:, LANES * column : LANES * (column + 1)]
        pieces = [part[start : start + rows] for start in range(0, span, rows)]
        base = ranks + rows * column
        out[base : base + rows] = jnp.concatenate(pieces, axis=1)


def pack(place, v_bases, x_in, first):
    _, _, parts, sources, ranks = v_bases.shape
    width = SIDE * parts * sources
    rows = ranks + parts * sources * FIRST // width
    tile_spec = lambda second: pl.BlockSpec(
        (1, 1, parts, sources, ranks), lambda i, place: (0, tile_at(place, first, second), 0, 0, 0)
    )
    return call(
        pack_kernel,
        jax.ShapeDtypeStruct((rows, width), jnp.float32),
        limit=PACK_LIMIT,
        grid_spec=pltpu.PrefetchScalarGridSpec(
            num_scalar_prefetch=1,
            grid=(1,),
            in_specs=[tile_spec(second) for second in range(SIDE)]
            + [pl.BlockSpec((1, parts, sources, FIRST), lambda i, place: (0, 0, 0, 0))],
            out_specs=pl.BlockSpec((rows, width), lambda i, place: (0, 0)),
        ),
    )(place, *[v_bases] * SIDE, x_in)


def coefficient_kernel(ranks, start, width, *refs):
    packed = refs[:SIDE]
    waves = refs[SIDE:-SIDE]
    outs = refs[-SIDE:]
    for first in range(SIDE):
        rows = packed[first][...]
        span = rows.shape[1] // SIDE
        if waves:
            wave = waves[first][...].reshape(span, -1)
        else:
            height = span * LANES // rows.shape[1]
            columns = []
            begin = ranks + height * start // LANES
            for base in range(begin, begin + height * width // LANES, height):
                tail = rows[base : base + height]
                pieces = [tail[:, at : at + LANES] for at in range(0, rows.shape[1], LANES)]
                columns.append(jnp.concatenate(pieces, axis=0))
            wave = jnp.concatenate(columns, axis=1)
        real, imag = wave[: span // 2], wave[span // 2 :]
        right = jnp.concatenate(
            [jnp.concatenate([real, imag], axis=1), jnp.concatenate([imag, -real], axis=1)], axis=0
        )
        left = jnp.concatenate(
            [rows[:ranks, span * second : span * (second + 1)] for second in range(SIDE)], axis=0
        )
        result = dot_split(split(left), split(right))
        for second in range(SIDE):
            outs[second][first] = result[ranks * second : ranks * (second + 1)]


def looped_kernel(ranks, *refs):
    packed, waves = refs[:SIDE], refs[SIDE : 2 * SIDE]
    outs, rows, wave = refs[2 * SIDE : 3 * SIDE], refs[-2], refs[-1]
    step = pl.program_id(0)
    for first in range(SIDE):

        @pl.when(step == first)
        def _():
            rows[...] = packed[first][:ranks]
            wave[...] = waves[first][...].reshape(wave.shape)

    span = wave.shape[0]
    real, imag = wave[: span // 2], wave[span // 2 :]
    right = jnp.concatenate(
        [jnp.concatenate([real, imag], axis=1), jnp.concatenate([imag, -real], axis=1)], axis=0
    )
    whole = rows[...]
    left = jnp.concatenate(
        [whole[:, span * second : span * (second + 1)] for second in range(SIDE)], axis=0
    )
    result = dot_split(split(left), split(right))
    for second in range(SIDE):
        outs[second][step] = result[ranks * second : ranks * (second + 1)]


def coefficients(packed, waves, ranks, start, width):
    rows, span = packed[0].shape
    sources = span // SIDE
    in_specs = [pl.BlockSpec((rows, span), lambda i: (0, 0))] * SIDE
    if waves:
        block = start // width
        in_specs += [pl.BlockSpec((2, sources // 2, width), lambda i: (0, 0, block))] * SIDE
    shape = (SIDE, ranks, 2 * width)
    extra = {}
    kernel = functools.partial(coefficient_kernel, ranks, start, width)
    if waves:
        kernel = functools.partial(looped_kernel, ranks)
        scratch = ((ranks, span), (2 * (sources // 2), width))
        extra["scratch_shapes"] = [pltpu.VMEM(size, jnp.float32) for size in scratch]
    return call(
        kernel,
        [jax.ShapeDtypeStruct(shape, jnp.float32)] * SIDE,
        flops=2 * 3 * SIDE * SIDE * ranks * sources * 2 * width,
        moved=4 << 20,
        grid=(SIDE if waves else 1,),
        in_specs=in_specs,
        out_specs=[pl.BlockSpec(shape, lambda i: (0, 0, 0))] * SIDE,
        **extra,
    )(*packed, *waves)


def bases_kernel(place, rank_table, *refs):
    tiles, out = refs[:SIDE], refs[SIDE]
    second = pl.program_id(0)
    for part in range(2):
        blocks = []
        for first in range(SIDE):
            block = tiles[first][0, 0, part]
            live = rank_table[place[6], tile_at(place, -first, -second)]
            index = lax.broadcasted_iota(jnp.int32, block.shape, 0)
            blocks.append(jnp.where(index < live, block, jnp.zeros_like(block)))
        turned = jnp.concatenate(blocks, axis=0).T
        out[0, part], out[1, part] = split(turned)


def receiver_bases(place, rank_table, u_bases):
    _, _, parts, ranks, receivers = u_bases.shape
    tile_spec = lambda first: pl.BlockSpec(
        (1, 1, parts, ranks, receivers),
        lambda second, place, table: (0, tile_at(place, -first, -second), 0, 0, 0),
    )
    shape = jax.ShapeDtypeStruct((2, parts, receivers, SIDE * SIDE * ranks), jnp.bfloat16)
    out_spec = pl.BlockSpec(
        (2, parts, receivers, SIDE * ranks), lambda second, place, table: (0, 0, 0, second)
    )
    return call(
        bases_kernel,
        shape,
        moved=12 << 20,
        grid_spec=pltpu.PrefetchScalarGridSpec(
            num_scalar_prefetch=2,
            grid=(SIDE,),
            in_specs=[tile_spec(first) for first in range(SIDE)],
            out_specs=out_spec,
        ),
    )(place, rank_table, *[u_bases] * SIDE)


def field_kernel(place, *refs):
    arrived = refs[:SIDE]
    bases, keep, send, right_high, right_low = refs[SIDE:]
    step = pl.program_id(0)

    @pl.when(step == 0)
    def _():
        for second in range(SIDE):
            block = arrived[second][...]
            rows = block.shape[0] * block.shape[1]
            high, low = split(block.reshape(rows, block.shape[2]))
            right_high[second * rows : (second + 1) * rows] = high
            right_low[second * rows : (second + 1) * rows] = low

    _, parts, receivers, depth = bases.shape
    rows = parts * receivers
    left = bases[...].reshape(2 * rows, depth)
    product = dot(left, right_high[...])
    product = product[:rows] + (product[rows:] + dot(left[:rows], right_low[...]))
    width = product.shape[1] // 2
    upper, lower = product[:receivers], product[receivers:]
    real = upper[:, :width] - lower[:, width:]
    imag = upper[:, width:] + lower[:, :width]
    share = keep.shape[2]
    own = place[4] == 0
    for local in range(receivers // (2 * share)):
        slot = (step * (receivers // (2 * share)) + local - place[5]) & (RING - 1)
        for part, value in enumerate((real, imag)):
            even = value[2 * share * local : 2 * share * local + share]
            odd = value[2 * share * local + share : 2 * share * (local + 1)]
            keep[slot, part] = jnp.where(own, even, odd)
            send[slot, part] = jnp.where(own, odd, even)


def field(place, arrived, bases):
    _, parts, receivers, depth = bases.shape
    columns = arrived[0].shape[2]
    share = receivers // (2 * RING)
    steps = columns // (2 * LANES)
    shape = (RING, 2, share, columns // 2)
    return call(
        field_kernel,
        [jax.ShapeDtypeStruct(shape, jnp.float32)] * 2,
        flops=2 * 3 * parts * receivers * depth * columns,
        moved=9 << 20,
        grid_spec=pltpu.PrefetchScalarGridSpec(
            num_scalar_prefetch=1,
            grid=(steps,),
            in_specs=[pl.BlockSpec(arrived[0].shape, lambda i, place: (0, 0, 0))] * SIDE
            + [pl.BlockSpec((2, parts, receivers // steps, depth), lambda i, place: (0, 0, i, 0))],
            out_specs=[pl.BlockSpec(shape, lambda i, place: (0, 0, 0, 0))] * 2,
            scratch_shapes=[pltpu.VMEM((depth, columns), jnp.bfloat16)] * 2,
        ),
    )(place, *arrived, bases)


def regroup_kernel(*refs):
    fields, outs = refs[:-RING], refs[-RING:]
    for turn, out in enumerate(outs):
        start = 0
        for index in range(0, len(fields), 2):
            width = fields[index].shape[3]
            for other in range(2):
                out[other, :, :, start : start + width] = fields[index + other][turn]
            start += width


def regroup(fields):
    width = sum(array.shape[3] for array in fields) // 2
    shape = (2,) + fields[0].shape[1:3] + (width,)
    return call(
        regroup_kernel,
        [jax.ShapeDtypeStruct(shape, jnp.float32)] * RING,
        grid=(1,),
        in_specs=[pl.BlockSpec(array.shape, lambda i: (0, 0, 0, 0)) for array in fields],
        out_specs=[pl.BlockSpec(shape, lambda i: (0, 0, 0, 0))] * RING,
    )(*fields)


def spread(table):
    rows, columns = table.shape
    shape = (columns, GROUP * columns)
    index = lax.broadcasted_iota(jnp.int32, shape, 1) // GROUP
    chosen = lax.broadcasted_iota(jnp.int32, shape, 0) == index
    wide = dot(table, chosen.astype(jnp.float32).astype(jnp.bfloat16))
    wide = jnp.broadcast_to(wide[:, None], (rows, GROUP, GROUP * columns))
    wide = wide.reshape(rows * GROUP, GROUP * columns)
    row = lax.broadcasted_iota(jnp.int32, wide.shape, 0)
    column = lax.broadcasted_iota(jnp.int32, wide.shape, 1)
    return jnp.where((row & (GROUP - 1)) == (column & (GROUP - 1)), wide, 0.0)


def table_kernel(high, low, high_turned, low_turned, inverse, forward):
    for parity in range(2):
        first = (spread(high[parity]) * (2.0 / NT)).astype(jnp.bfloat16)
        second = (spread(low[parity]) * (2.0 / NT)).astype(jnp.bfloat16)
        inverse[parity] = jnp.concatenate([first, second, first], axis=1)
        first = spread(high_turned[parity]).astype(jnp.bfloat16)
        second = spread(low_turned[parity]).astype(jnp.bfloat16)
        block = forward.shape[3] // 3
        for index in range(forward.shape[1]):
            at = slice(block * index, block * (index + 1))
            pieces = [first[:, at], second[:, at], first[:, at]]
            forward[parity, index] = jnp.concatenate(pieces, axis=1)


def mute_tables(freq_count):
    sample = np.arange(HALF)[:, None]
    cycle = FLOW // FSTEP + np.arange(freq_count)[None, :]
    angles = (sample * cycle % PERIOD) * (2.0 * math.pi / PERIOD)
    table = np.stack([np.cos(angles), -np.sin(angles)], axis=2)
    table = table.reshape(HALF, freq_count // 2, 2, 2).transpose(2, 0, 1, 3)
    table = table.reshape(2, HALF, freq_count).astype(np.float32)
    high = table.astype(jnp.bfloat16)
    low = (table - high.astype(np.float32)).astype(jnp.bfloat16)
    turn = lambda array: np.ascontiguousarray(array.transpose(0, 2, 1))
    parts = [jnp.asarray(part) for part in (high, low, turn(high), turn(low))]
    rows = freq_count * GROUP
    shapes = ((2, HALF * GROUP, 3 * rows), (2, 2, rows, 3 * HALF * GROUP // 2))
    return call(
        table_kernel, [jax.ShapeDtypeStruct(shape, jnp.bfloat16) for shape in shapes], moved=2 << 20
    )(*parts)


def mute_kernel(place, *refs):
    pieces = refs[:RING]
    mute, inverse, forward = refs[RING : RING + 3]
    out, gathered = refs[-2:]
    for step in range(RING):
        ring = (place[5] - step) & (RING - 1)
        for other in range(2):
            parity = place[4] ^ other
            for group in range(2):
                value = pieces[step][other, :, GROUP * group : GROUP * (group + 1)]
                gathered[group, parity, ring] = value
    _, blocks, rows, _ = forward.shape
    span = HALF * GROUP // blocks
    samples = HALF // blocks
    limit = jnp.concatenate([mute[:GROUP], mute[GROUP:]], axis=1)[None]

    def stacked(value):
        high, low = split(value)
        return jnp.concatenate([high, high, low], axis=0)

    def count(sample):
        live = (limit - sample + (PERIOD - 1)) >> (PERIOD.bit_length() - 1)
        return live.astype(jnp.float32)

    waves = []
    for parity in range(2):
        columns = [gathered[group, parity].reshape(rows, LANES) for group in range(2)]
        waves.append(dot(inverse[parity], stacked(jnp.concatenate(columns, axis=1))))
    results = [None, None]
    for block in range(blocks):
        shape = (samples, GROUP, 2 * LANES)
        even, odd = [wave[span * block : span * (block + 1)].reshape(shape) for wave in waves]
        sample = lax.broadcasted_iota(jnp.int32, shape, 0) + samples * block
        near = (odd + even) * count(sample)
        far = (odd - even) * count(sample + HALF)
        for parity, value in enumerate((near - far, near + far)):
            term = dot(forward[parity, block], stacked(value.reshape(span, 2 * LANES)))
            results[parity] = term if block == 0 else results[parity] + term
    for parity in range(2):
        for group in range(2):
            part = results[parity][:, LANES * group : LANES * (group + 1)]
            part = part.reshape(RING, 2, GROUP, LANES)
            for ring in range(RING):
                out[2 * ring + parity, :, GROUP * group : GROUP * (group + 1)] = part[ring]


def time_mute(place, pieces, mute_rows, tables, start, before):
    _, parts, receivers, width = pieces[0].shape
    points = mute_rows.shape[1]
    freqs = 2 * RING
    offset = start // LANES
    whole = lambda shape: pl.BlockSpec(shape, lambda j, h, place: (0,) * len(shape))
    in_specs = [pl.BlockSpec((2, parts, 2 * GROUP, LANES), lambda j, h, place: (0, 0, h, j))] * RING
    in_specs += [pl.BlockSpec((2 * GROUP, LANES), lambda j, h, place: (h, offset + j))]
    in_specs += [whole(table.shape) for table in tables]
    operands = [place, *pieces, mute_rows, *tables]
    aliases = {}
    if before is not None:
        aliases = {len(operands): 0}
        in_specs += [pl.BlockSpec(memory_space=pl.ANY)]
        operands += [before]
    return call(
        mute_kernel,
        jax.ShapeDtypeStruct((freqs, parts, receivers, points), jnp.float32),
        flops=2 * 2 * tables[0].size * (receivers // GROUP) * width,
        moved=4 << 20,
        grid_spec=pltpu.PrefetchScalarGridSpec(
            num_scalar_prefetch=1,
            grid=(width // LANES, receivers // (2 * GROUP)),
            in_specs=in_specs,
            out_specs=pl.BlockSpec(
                (freqs, parts, 2 * GROUP, LANES), lambda j, h, place: (0, 0, h, offset + j)
            ),
            scratch_shapes=[pltpu.VMEM((2, 2, RING, parts, GROUP, LANES), jnp.float32)],
        ),
        input_output_aliases=aliases,
    )(*operands)


def step(x_in, v_bases, u_bases, ranks, mute):
    place = place_of_device()
    rank_count = v_bases.shape[3]
    v_bases = jnp.swapaxes(v_bases, 3, 4)
    order = SIDE_ORDER
    packed = {first: pack(place, v_bases, x_in, first) for first in order + (0,)}
    near = {0: packed[0]}
    for first in order:
        near[first] = plane_shift(packed[first], first, 0)
    rest = x_in[0, :, :, FIRST:]
    rests = {0: rest}
    for first in order:
        rests[first] = plane_shift(rest, first, 0)
    bases = receiver_bases(place, ranks[0], u_bases)
    tables = mute_tables(2 * RING)
    inputs = [near[first] for first in range(SIDE)]
    waves = [rests[first] for first in range(SIDE)]
    result = None
    chunk = start = done = 0
    for batch, widths in enumerate(BATCHES):
        fields = []
        for width in widths:
            shown = waves if batch else []
            offset = start - FIRST if batch else start
            blocks = coefficients(inputs, shown, rank_count, offset, width)
            arrived = {0: blocks[0]}
            for second in order:
                arrived[second] = plane_shift(blocks[second], 0, second)
            keep, send = field(place, [arrived[second] for second in range(SIDE)], bases)
            fields += [keep, ring_shift(send, 0, 1)]
            chunk += 1
            start += width
        pieces = regroup(fields)
        landed = {0: pieces[0]}
        for turn in RING_ORDER:
            landed[turn] = ring_shift(pieces[turn], turn, 0)
        result = time_mute(
            place, [landed[turn] for turn in range(RING)], mute[0], tables, done, result
        )
        done = start
    return result[None]


def solution(mesh):
    placed = (
        P("freq", None, "tile", None),
        P("freq", None, None, None, "tile"),
        P("freq", None, None, None, "tile"),
        P("freq", None, None),
        P("tile", "freq", None),
    )
    return jax.shard_map(
        step,
        mesh=mesh,
        in_specs=placed,
        out_specs=P("tile", None, None, "freq", None),
        check_vma=False,
    )
```

```python
import functools
import math

import jax
import jax.numpy as jnp
import numpy as np
from jax import lax
from jax.experimental import pallas as pl
from jax.experimental.pallas import tpu as pltpu
from jax.sharding import PartitionSpec as P


NT = 512
FLOW = 20
FSTEP = 4
PERIOD = NT // FSTEP
HALF = PERIOD // 2
GROUP = 8
SIDE = 4
SIDE_ORDER = (1, 3, 2)
PACK_LIMIT = 18
RING = 8
LANES = 128
BATCHES = ((128, 128), (256,))
RING_ORDERS = ((1, 7, 4, 3, 5, 2, 6), (4, 3, 5, 2, 6, 1, 7))
FIRST = sum(BATCHES[0])


def split(value):
    high = value.astype(jnp.bfloat16)
    low = (value - high.astype(jnp.float32)).astype(jnp.bfloat16)
    return high, low


def dot(left, right):
    return jnp.dot(left, right, preferred_element_type=jnp.float32)


def dot_split(left, right):
    return dot(left[0], right[0]) + (dot(left[0], right[1]) + dot(left[1], right[0]))


def call(kernel, out_shape, flops=0, moved=1 << 20, limit=18, **kwargs):
    return pl.pallas_call(
        kernel,
        out_shape=out_shape,
        compiler_params=pltpu.CompilerParams(vmem_limit_bytes=limit << 20),
        cost_estimate=pl.CostEstimate(flops=flops, bytes_accessed=moved, transcendentals=0),
        **kwargs,
    )


def place_of_device():
    tile = lax.axis_index("tile")
    freq = lax.axis_index("freq")
    core = freq % 2
    straight = core == 0
    high, low = tile // SIDE, tile % SIDE
    values = (
        jnp.where(straight, high, low),
        jnp.where(straight, low, high),
        jnp.where(straight, SIDE, 1),
        jnp.where(straight, 1, SIDE),
        core,
        freq // 2,
        tile,
    )
    slot = lax.broadcasted_iota(jnp.int32, (8,), 0)
    place = jnp.zeros((8,), jnp.int32)
    for index, value in enumerate(values):
        place = jnp.where(slot == index, value.astype(jnp.int32), place)
    return place


def tile_at(place, first, second):
    return ((place[0] + first) & (SIDE - 1)) * place[2] + ((place[1] + second) & (SIDE - 1)) * place[3]


def plane_shift(array, first, second):
    pairs = []
    for freq in range(2 * RING):
        strides = (SIDE, 1) if freq % 2 == 0 else (1, SIDE)
        for one in range(SIDE):
            for two in range(SIDE):
                source = one * strides[0] + two * strides[1]
                target = (one + first) % SIDE * strides[0] + (two + second) % SIDE * strides[1]
                pairs.append((freq * SIDE * SIDE + source, freq * SIDE * SIDE + target))
    return lax.ppermute(array, ("freq", "tile"), pairs)


def ring_shift(array, step, swap):
    pairs = [
        (z * 2 + core, (z + step) % RING * 2 + (core + swap) % 2)
        for z in range(RING)
        for core in range(2)
    ]
    return lax.ppermute(array, "freq", pairs)


def pack_kernel(place, *refs):
    tiles, x_ref, out = refs[:SIDE], refs[SIDE], refs[SIDE + 1]
    ranks = tiles[0].shape[4]
    blocks = [tile[0, 0, part].T for tile in tiles for part in range(2)]
    out[:ranks] = jnp.concatenate(blocks, axis=1)
    span = out.shape[1] // SIDE
    rows = span * LANES // out.shape[1]
    wave = x_ref[0].reshape(span, -1)
    for column in range(wave.shape[1] // LANES):
        part = wave[:, LANES * column : LANES * (column + 1)]
        pieces = [part[start : start + rows] for start in range(0, span, rows)]
        base = ranks + rows * column
        out[base : base + rows] = jnp.concatenate(pieces, axis=1)


def pack(place, v_bases, x_in, first):
    _, _, parts, sources, ranks = v_bases.shape
    width = SIDE * parts * sources
    rows = ranks + parts * sources * FIRST // width
    tile_spec = lambda second: pl.BlockSpec(
        (1, 1, parts, sources, ranks), lambda i, place: (0, tile_at(place, first, second), 0, 0, 0)
    )
    return call(
        pack_kernel,
        jax.ShapeDtypeStruct((rows, width), jnp.float32),
        limit=PACK_LIMIT,
        grid_spec=pltpu.PrefetchScalarGridSpec(
            num_scalar_prefetch=1,
            grid=(1,),
            in_specs=[tile_spec(second) for second in range(SIDE)]
            + [pl.BlockSpec((1, parts, sources, FIRST), lambda i, place: (0, 0, 0, 0))],
            out_specs=pl.BlockSpec((rows, width), lambda i, place: (0, 0)),
        ),
    )(place, *[v_bases] * SIDE, x_in)


def coefficient_kernel(ranks, start, width, *refs):
    packed = refs[:SIDE]
    waves = refs[SIDE:-SIDE]
    outs = refs[-SIDE:]
    for first in range(SIDE):
        rows = packed[first][...]
        span = rows.shape[1] // SIDE
        if waves:
            wave = waves[first][...].reshape(span, -1)
        else:
            height = span * LANES // rows.shape[1]
            columns = []
            begin = ranks + height * start // LANES
            for base in range(begin, begin + height * width // LANES, height):
                tail = rows[base : base + height]
                pieces = [tail[:, at : at + LANES] for at in range(0, rows.shape[1], LANES)]
                columns.append(jnp.concatenate(pieces, axis=0))
            wave = jnp.concatenate(columns, axis=1)
        real, imag = wave[: span // 2], wave[span // 2 :]
        right = jnp.concatenate(
            [jnp.concatenate([real, imag], axis=1), jnp.concatenate([imag, -real], axis=1)], axis=0
        )
        left = jnp.concatenate(
            [rows[:ranks, span * second : span * (second + 1)] for second in range(SIDE)], axis=0
        )
        result = dot_split(split(left), split(right))
        for second in range(SIDE):
            outs[second][first] = result[ranks * second : ranks * (second + 1)]


def looped_kernel(ranks, *refs):
    packed, waves = refs[:SIDE], refs[SIDE : 2 * SIDE]
    outs, rows, wave = refs[2 * SIDE : 3 * SIDE], refs[-2], refs[-1]
    step = pl.program_id(0)
    for first in range(SIDE):

        @pl.when(step == first)
        def _():
            rows[...] = packed[first][:ranks]
            wave[...] = waves[first][...].reshape(wave.shape)

    span = wave.shape[0]
    real, imag = wave[: span // 2], wave[span // 2 :]
    right = jnp.concatenate(
        [jnp.concatenate([real, imag], axis=1), jnp.concatenate([imag, -real], axis=1)], axis=0
    )
    whole = rows[...]
    left = jnp.concatenate(
        [whole[:, span * second : span * (second + 1)] for second in range(SIDE)], axis=0
    )
    result = dot_split(split(left), split(right))
    for second in range(SIDE):
        outs[second][step] = result[ranks * second : ranks * (second + 1)]


def coefficients(packed, waves, ranks, start, width):
    rows, span = packed[0].shape
    sources = span // SIDE
    in_specs = [pl.BlockSpec((rows, span), lambda i: (0, 0))] * SIDE
    if waves:
        block = start // width
        in_specs += [pl.BlockSpec((2, sources // 2, width), lambda i: (0, 0, block))] * SIDE
    shape = (SIDE, ranks, 2 * width)
    extra = {}
    kernel = functools.partial(coefficient_kernel, ranks, start, width)
    if waves:
        kernel = functools.partial(looped_kernel, ranks)
        scratch = ((ranks, span), (2 * (sources // 2), width))
        extra["scratch_shapes"] = [pltpu.VMEM(size, jnp.float32) for size in scratch]
    return call(
        kernel,
        [jax.ShapeDtypeStruct(shape, jnp.float32)] * SIDE,
        flops=2 * 3 * SIDE * SIDE * ranks * sources * 2 * width,
        moved=4 << 20,
        grid=(SIDE if waves else 1,),
        in_specs=in_specs,
        out_specs=[pl.BlockSpec(shape, lambda i: (0, 0, 0))] * SIDE,
        **extra,
    )(*packed, *waves)


def bases_kernel(place, rank_table, *refs):
    tiles, out = refs[:SIDE], refs[SIDE]
    second = pl.program_id(0)
    for part in range(2):
        blocks = []
        for first in range(SIDE):
            block = tiles[first][0, 0, part]
            live = rank_table[place[6], tile_at(place, -first, -second)]
            index = lax.broadcasted_iota(jnp.int32, block.shape, 0)
            blocks.append(jnp.where(index < live, block, jnp.zeros_like(block)))
        turned = jnp.concatenate(blocks, axis=0).T
        out[0, part], out[1, part] = split(turned)


def receiver_bases(place, rank_table, u_bases):
    _, _, parts, ranks, receivers = u_bases.shape
    tile_spec = lambda first: pl.BlockSpec(
        (1, 1, parts, ranks, receivers),
        lambda second, place, table: (0, tile_at(place, -first, -second), 0, 0, 0),
    )
    shape = jax.ShapeDtypeStruct((2, parts, receivers, SIDE * SIDE * ranks), jnp.bfloat16)
    out_spec = pl.BlockSpec(
        (2, parts, receivers, SIDE * ranks), lambda second, place, table: (0, 0, 0, second)
    )
    return call(
        bases_kernel,
        shape,
        moved=12 << 20,
        grid_spec=pltpu.PrefetchScalarGridSpec(
            num_scalar_prefetch=2,
            grid=(SIDE,),
            in_specs=[tile_spec(first) for first in range(SIDE)],
            out_specs=out_spec,
        ),
    )(place, rank_table, *[u_bases] * SIDE)


def field_kernel(place, *refs):
    arrived = refs[:SIDE]
    bases, keep, send, right_high, right_low = refs[SIDE:]
    step = pl.program_id(0)

    @pl.when(step == 0)
    def _():
        for second in range(SIDE):
            block = arrived[second][...]
            rows = block.shape[0] * block.shape[1]
            high, low = split(block.reshape(rows, block.shape[2]))
            right_high[second * rows : (second + 1) * rows] = high
            right_low[second * rows : (second + 1) * rows] = low

    _, parts, receivers, depth = bases.shape
    rows = parts * receivers
    left = bases[...].reshape(2 * rows, depth)
    product = dot(left, right_high[...])
    product = product[:rows] + (product[rows:] + dot(left[:rows], right_low[...]))
    width = product.shape[1] // 2
    upper, lower = product[:receivers], product[receivers:]
    real = upper[:, :width] - lower[:, width:]
    imag = upper[:, width:] + lower[:, :width]
    share = keep.shape[2]
    own = place[4] == 0
    for local in range(receivers // (2 * share)):
        slot = (step * (receivers // (2 * share)) + local - place[5]) & (RING - 1)
        for part, value in enumerate((real, imag)):
            even = value[2 * share * local : 2 * share * local + share]
            odd = value[2 * share * local + share : 2 * share * (local + 1)]
            keep[slot, part] = jnp.where(own, even, odd)
            send[slot, part] = jnp.where(own, odd, even)


def field(place, arrived, bases):
    _, parts, receivers, depth = bases.shape
    columns = arrived[0].shape[2]
    share = receivers // (2 * RING)
    steps = columns // (2 * LANES)
    shape = (RING, 2, share, columns // 2)
    return call(
        field_kernel,
        [jax.ShapeDtypeStruct(shape, jnp.float32)] * 2,
        flops=2 * 3 * parts * receivers * depth * columns,
        moved=9 << 20,
        grid_spec=pltpu.PrefetchScalarGridSpec(
            num_scalar_prefetch=1,
            grid=(steps,),
            in_specs=[pl.BlockSpec(arrived[0].shape, lambda i, place: (0, 0, 0))] * SIDE
            + [pl.BlockSpec((2, parts, receivers // steps, depth), lambda i, place: (0, 0, i, 0))],
            out_specs=[pl.BlockSpec(shape, lambda i, place: (0, 0, 0, 0))] * 2,
            scratch_shapes=[pltpu.VMEM((depth, columns), jnp.bfloat16)] * 2,
        ),
    )(place, *arrived, bases)


def regroup_kernel(*refs):
    fields, outs = refs[:-RING], refs[-RING:]
    for turn, out in enumerate(outs):
        start = 0
        for index in range(0, len(fields), 2):
            width = fields[index].shape[3]
            for other in range(2):
                out[other, :, :, start : start + width] = fields[index + other][turn]
            start += width


def regroup(fields):
    width = sum(array.shape[3] for array in fields) // 2
    shape = (2,) + fields[0].shape[1:3] + (width,)
    return call(
        regroup_kernel,
        [jax.ShapeDtypeStruct(shape, jnp.float32)] * RING,
        grid=(1,),
        in_specs=[pl.BlockSpec(array.shape, lambda i: (0, 0, 0, 0)) for array in fields],
        out_specs=[pl.BlockSpec(shape, lambda i: (0, 0, 0, 0))] * RING,
    )(*fields)


def spread(table):
    rows, columns = table.shape
    shape = (columns, GROUP * columns)
    index = lax.broadcasted_iota(jnp.int32, shape, 1) // GROUP
    chosen = lax.broadcasted_iota(jnp.int32, shape, 0) == index
    wide = dot(table, chosen.astype(jnp.float32).astype(jnp.bfloat16))
    wide = jnp.broadcast_to(wide[:, None], (rows, GROUP, GROUP * columns))
    wide = wide.reshape(rows * GROUP, GROUP * columns)
    row = lax.broadcasted_iota(jnp.int32, wide.shape, 0)
    column = lax.broadcasted_iota(jnp.int32, wide.shape, 1)
    return jnp.where((row & (GROUP - 1)) == (column & (GROUP - 1)), wide, 0.0)


def table_kernel(high, low, high_turned, low_turned, inverse, forward):
    first = (spread(high[0]) * (2.0 / NT)).astype(jnp.bfloat16)
    second = (spread(low[0]) * (2.0 / NT)).astype(jnp.bfloat16)
    both = jnp.concatenate([first, second], axis=0)
    inverse[0] = jnp.concatenate([both, both], axis=1)
    first = spread(high_turned[0]).astype(jnp.bfloat16)
    second = spread(low_turned[0]).astype(jnp.bfloat16)
    both = jnp.concatenate([first, second], axis=0)
    block = forward.shape[3] // 2
    for index in range(forward.shape[1]):
        piece = both[:, block * index : block * (index + 1)]
        forward[0, index] = jnp.concatenate([piece, piece], axis=1)


def mute_tables(freq_count):
    sample = np.arange(HALF)[:, None]
    cycle = FLOW // FSTEP + np.arange(freq_count)[None, :]
    angles = (sample * cycle % PERIOD) * (2.0 * math.pi / PERIOD)
    table = np.stack([np.cos(angles), -np.sin(angles)], axis=2)
    table = table.reshape(HALF, freq_count // 2, 2, 2).transpose(2, 0, 1, 3)
    table = table.reshape(2, HALF, freq_count).astype(np.float32)
    high = table.astype(jnp.bfloat16)
    low = (table - high.astype(np.float32)).astype(jnp.bfloat16)
    turn = lambda array: np.ascontiguousarray(array.transpose(0, 2, 1))
    parts = [jnp.asarray(part) for part in (high, low, turn(high), turn(low))]
    half = lambda size: pl.BlockSpec((1,) + size[1:], lambda i: (i,) + (0,) * (len(size) - 1))
    rows = freq_count * GROUP
    shapes = ((2, 2 * HALF * GROUP, 2 * rows), (2, 2, 2 * rows, HALF * GROUP))
    return call(
        table_kernel,
        [jax.ShapeDtypeStruct(shape, jnp.bfloat16) for shape in shapes],
        moved=2 << 20,
        grid=(2,),
        in_specs=[half(part.shape) for part in parts],
        out_specs=[half(shape) for shape in shapes],
    )(*parts)


def mute_kernel(place, *refs):
    pieces = refs[:RING]
    mute, inverse, forward = refs[RING : RING + 3]
    out, gathered = refs[-2:]
    groups = gathered.shape[0]
    for step in range(RING):
        ring = (place[5] - step) & (RING - 1)
        for other in range(2):
            parity = place[4] ^ other
            for group in range(groups):
                value = pieces[step][other, :, GROUP * group : GROUP * (group + 1)]
                gathered[group, parity, ring] = value
    _, blocks, rows, _ = forward.shape
    rows //= 2
    span = HALF * GROUP // blocks
    samples = HALF // blocks
    limit = jnp.concatenate(
        [mute[GROUP * group : GROUP * (group + 1)] for group in range(groups)], axis=1
    )[None]

    def stacked(value):
        high, low = split(value)
        return jnp.concatenate([high, low], axis=0)

    def folded(value):
        half = value.shape[0] // 2
        return value[:half] + value[half:]

    def count(sample):
        live = (limit - sample + (PERIOD - 1)) >> (PERIOD.bit_length() - 1)
        return live.astype(jnp.float32)

    waves = []
    for parity in range(2):
        columns = [gathered[group, parity].reshape(rows, LANES) for group in range(groups)]
        waves.append(folded(dot(inverse[parity], stacked(jnp.concatenate(columns, axis=1)))))
    results = [None, None]
    for block in range(blocks):
        shape = (samples, GROUP, groups * LANES)
        even, odd = [wave[span * block : span * (block + 1)].reshape(shape) for wave in waves]
        sample = lax.broadcasted_iota(jnp.int32, shape, 0) + samples * block
        near = (odd + even) * count(sample)
        far = (odd - even) * count(sample + HALF)
        for parity, value in enumerate((near - far, near + far)):
            term = dot(forward[parity, block], stacked(value.reshape(span, groups * LANES)))
            results[parity] = term if block == 0 else results[parity] + term
    for parity in range(2):
        for group in range(groups):
            part = folded(results[parity][:, LANES * group : LANES * (group + 1)])
            part = part.reshape(RING, 2, GROUP, LANES)
            for ring in range(RING):
                out[2 * ring + parity, :, GROUP * group : GROUP * (group + 1)] = part[ring]


def time_mute(place, pieces, mute_rows, tables, start, before, groups):
    _, parts, receivers, width = pieces[0].shape
    points = mute_rows.shape[1]
    freqs = 2 * RING
    offset = start // LANES
    whole = lambda shape: pl.BlockSpec(shape, lambda j, h, place: (0,) * len(shape))
    in_specs = [pl.BlockSpec((2, parts, groups * GROUP, LANES), lambda j, h, place: (0, 0, h, j))] * RING
    in_specs += [pl.BlockSpec((groups * GROUP, LANES), lambda j, h, place: (h, offset + j))]
    in_specs += [whole(table.shape) for table in tables]
    operands = [place, *pieces, mute_rows, *tables]
    aliases = {}
    if before is not None:
        aliases = {len(operands): 0}
        in_specs += [pl.BlockSpec(memory_space=pl.ANY)]
        operands += [before]
    return call(
        mute_kernel,
        jax.ShapeDtypeStruct((freqs, parts, receivers, points), jnp.float32),
        flops=2 * 2 * tables[0].size * (receivers // GROUP) * width,
        moved=4 << 20,
        grid_spec=pltpu.PrefetchScalarGridSpec(
            num_scalar_prefetch=1,
            grid=(width // LANES, receivers // (groups * GROUP)),
            in_specs=in_specs,
            out_specs=pl.BlockSpec(
                (freqs, parts, groups * GROUP, LANES), lambda j, h, place: (0, 0, h, offset + j)
            ),
            scratch_shapes=[pltpu.VMEM((groups, 2, RING, parts, GROUP, LANES), jnp.float32)],
        ),
        input_output_aliases=aliases,
    )(*operands)


def step(x_in, v_bases, u_bases, ranks, mute):
    place = place_of_device()
    rank_count = v_bases.shape[3]
    v_bases = jnp.swapaxes(v_bases, 3, 4)
    order = SIDE_ORDER
    first_points = lax.optimization_barrier(x_in[..., :FIRST])
    packed = {first: pack(place, v_bases, first_points, first) for first in order + (0,)}
    near = {0: packed[0]}
    for first in order:
        near[first] = plane_shift(packed[first], first, 0)
    rest = x_in[0, :, :, FIRST:]
    rests = {0: rest}
    for first in order:
        rests[first] = plane_shift(rest, first, 0)
    bases = receiver_bases(place, ranks[0], u_bases)
    tables = mute_tables(2 * RING)
    inputs = [near[first] for first in range(SIDE)]
    waves = [rests[first] for first in range(SIDE)]
    result = None
    chunk = start = done = 0
    for batch, widths in enumerate(BATCHES):
        fields = []
        for width in widths:
            shown = waves if batch else []
            offset = start - FIRST if batch else start
            blocks = coefficients(inputs, shown, rank_count, offset, width)
            arrived = {0: blocks[0]}
            for second in order:
                arrived[second] = plane_shift(blocks[second], 0, second)
            keep, send = field(place, [arrived[second] for second in range(SIDE)], bases)
            fields += [keep, ring_shift(send, 0, 1)]
            chunk += 1
            start += width
        pieces = regroup(fields)
        landed = {0: pieces[0]}
        for turn in RING_ORDERS[batch]:
            landed[turn] = ring_shift(pieces[turn], turn, 0)
        result = time_mute(
            place,
            [landed[turn] for turn in range(RING)],
            mute[0],
            tables,
            done,
            result,
            2,
        )
        done = start
    return result[None]


def solution(mesh):
    placed = (
        P("freq", None, "tile", None),
        P("freq", None, None, None, "tile"),
        P("freq", None, None, None, "tile"),
        P("freq", None, None),
        P("tile", "freq", None),
    )
    return jax.shard_map(
        step,
        mesh=mesh,
        in_specs=placed,
        out_specs=P("tile", None, None, "freq", None),
        check_vma=False,
    )
```
